32 devices in a mesh: dp: 2 (over y), expert: 4 (over x, core), tensor: 4 (over z).
Axes of the slice: x: 2, y: 2, z: 4, core: 2. Of those that a mesh axis runs over, the one named last changes fastest.
Arguments:
- hidden_states: bfloat16 [256, 4096], P(('dp', 'expert'), 'tensor'), may hold values from -6 to 6
- chosen_experts: int32 [256, 2], P(('dp', 'expert')), may hold values from 0 to 3, all different within a row; in each aligned block of 32 rows (0 to 31, 32 to 63, ...) at most 16 rows name the same one
- choice_weights: float32 [256, 2], P(('dp', 'expert')), may hold values from 0.2 to 1
- gate_proj: bfloat16 [4, 4096, 8192], P('expert', None, ('dp', 'tensor')), may hold values from -0.09375 to 0.09375
- up_proj: bfloat16 [4, 4096, 8192], P('expert', None, ('dp', 'tensor')), may hold values from -0.09375 to 0.09375
- down_proj: bfloat16 [4, 8192, 4096], P('expert', 'dp', 'tensor'), may hold values from -0.0625 to 0.0625
Outputs:
- moe_output: bfloat16 [256, 4096], P(('dp', 'expert'), 'tensor')
The draws below stay inside these ranges and needn't reach their ends.
Inputs may be any that keep to these rules, and one draw needn't show every extreme that they name: `chosen_experts`: each row names 2 different experts; among the 32 rows of one device no expert is named more than 16 times, a bound that some block reaches.
All inputs are finite; a program needn't handle non-finite values.
Results may differ from the reference program's by a relative error of at most 0.0058.
Values may be sent and summed in bfloat16 or wider, within the bound.
A program may use at most 64 MiB of HBM per device.

```python
import math
import jax
import jax.numpy as jnp
import numpy as np
from jax import lax

D = 4096
FF = 8192
TOP = 2
CAP = 16
TOK_DEV = 32
EXPERTS = 4
TOKENS = 256
N_DP = 2


def steps_of(stream_key, extent, pieces, least, largest):
    factor_of = 1.0
    for dim, parts in pieces:
        heights = jax.random.uniform(jax.random.fold_in(jax.random.fold_in(stream_key, 6), dim), (parts,), jnp.float32, least / len(pieces), largest / len(pieces))
        factor_of = factor_of * jnp.repeat(jnp.exp(heights), extent[dim] // parts).reshape((-1,) + (1,) * (len(extent) - 1 - dim))
    return factor_of


def assign_block(key, own, number, rows, number_of, top, bound, slope):
    order = jax.random.permutation(key, number_of)
    packed, common = shares(number_of, rows * top, bound, slope, True), shares(number_of, rows * top, bound, slope, False)
    places = jnp.arange(number_of)

    def named(sizes, offset_by):
        used = int((sizes > 0).sum())
        fixed = max(1, used // 4)
        passed = fixed + (places - fixed + offset_by * (used - fixed)) % max(1, number_of - fixed)
        return jnp.zeros((number_of,), jnp.int32).at[order[jnp.where(places < fixed, places, passed)]].set(jnp.asarray(sizes, jnp.int32))

    sizes = jnp.where(number % 4 == 0, named(packed, number // 4), named(common, number - number // 4 - 1))
    mixed = jax.random.permutation(jax.random.fold_in(own, 3), number_of)
    source_of, taker = mixed[0:number_of // 2 * 2:2], mixed[1:number_of // 2 * 2:2]
    room = jnp.minimum(sizes[source_of] - 1, bound - sizes[taker]) // 2
    room = jnp.where((source_of == order[0]) | (taker == order[0]) | (sizes[taker] == 0), 0, jnp.maximum(room, 0))
    passed = jax.random.randint(jax.random.fold_in(own, 4), (number_of // 2,), 0, 1 << 20) % (room + 1)
    sizes = sizes.at[source_of].add(-passed).at[taker].add(passed)
    items = jnp.searchsorted(jnp.cumsum(sizes), jnp.arange(rows * top), side="right").astype(jnp.int32)
    table = items.reshape(top, rows).T
    table = table[jax.random.permutation(jax.random.fold_in(own, 1), rows)]
    offset_by = jax.random.randint(jax.random.fold_in(own, 2), (rows, 1), 0, top)
    return jnp.take_along_axis(table, (jnp.arange(top)[None, :] + offset_by) % top, axis=1)


def shares(number_of, total, most, skew, full):
    weights = [(1 << 20) // math.isqrt(standing ** skew) + 1 for standing in range(1, number_of + 1)]
    largest = most if full else min(most, max(-(-total // number_of), total * weights[0] // sum(weights)))
    least = 1 if total - largest >= number_of - 1 else 0
    given, spare = [largest] + [least] * (number_of - 1), total - largest - least * (number_of - 1)
    while spare > 0:
        candidates = [i for i in range(1, number_of) if given[i] < largest] or [i for i in range(1, number_of) if given[i] < most]
        pool, remaining = sum([weights[i] for i in candidates]), spare
        for i in candidates:
            more = min(most - given[i], max(1, remaining * weights[i] // pool), spare)
            given[i] = given[i] + more
            spare = spare - more
    return np.array(given)


def centred(key, extent, deviation, limit, cuts=(), kind=jnp.bfloat16):
    array = jax.random.normal(key, extent, jnp.float32) * deviation
    if len(cuts) > 0:
        array = steps_of(key, extent, cuts, -0.22, 0.18) * array
    return jnp.clip(array, min=-limit, max=limit).astype(kind)


def setup_inputs(seed: int = 0) -> dict:
    key_of = jax.random.split(jax.random.key(seed), 7)
    hidden_states = centred(key_of[0], (TOKENS, D), 1.0, 6.0, ((0, 8), (1, 4)))
    chosen_experts_keys = jax.random.split(jax.random.fold_in(key_of[1], 1), TOKENS // TOK_DEV)
    chosen_experts_turns = jax.random.permutation(jax.random.fold_in(key_of[1], 3), TOKENS // TOK_DEV)
    chosen_experts = jax.vmap(lambda own, number: assign_block(jax.random.fold_in(key_of[1], 2), own, number, TOK_DEV, EXPERTS, TOP, CAP, 2))(chosen_experts_keys, chosen_experts_turns).reshape((TOKENS, TOP))
    choice_weights = jnp.clip(0.2 + 0.8 * jax.random.uniform(key_of[2], (TOKENS, TOP), jnp.float32) ** steps_of(key_of[2], (TOKENS, TOP), ((0, 8),), -0.2, 0.2), 0.2, 1.0)
    gate_proj = centred(key_of[3], (EXPERTS, D, FF), D ** -0.5, 0.09375, ((0, 4), (2, 8)))
    up_proj = centred(key_of[4], (EXPERTS, D, FF), D ** -0.5, 0.09375, ((0, 4), (2, 8)))
    down_proj = centred(key_of[5], (EXPERTS, FF, D), FF ** -0.5, 0.0625, ((0, 4), (1, 2), (2, 4)))
    return {"hidden_states": hidden_states, "chosen_experts": chosen_experts, "choice_weights": choice_weights, "gate_proj": gate_proj, "up_proj": up_proj, "down_proj": down_proj}


def reference(hidden_states, chosen_experts, choice_weights, gate_proj, up_proj, down_proj):
    row_limit = N_DP * EXPERTS * CAP

    def expert_step(totals, expert):
        picked = chosen_experts == expert
        chosen = jnp.any(picked, axis=1)
        weight_row = jnp.sum(jnp.where(picked, choice_weights, jnp.float32(0.0)), axis=1)
        ranking = jnp.where(chosen, 0, 1).astype(jnp.int32)
        order = jnp.argsort(ranking, stable=True)[:row_limit].astype(jnp.int32)
        gathered = hidden_states[order]
        gate_part = jnp.dot(gathered, gate_proj[expert], preferred_element_type=jnp.float32)
        up_part = jnp.dot(gathered, up_proj[expert], preferred_element_type=jnp.float32)
        activated = (jax.nn.silu(gate_part) * up_part).astype(jnp.bfloat16)
        out_rows = jnp.dot(activated, down_proj[expert], preferred_element_type=jnp.float32)
        out_rows = lax.optimization_barrier(out_rows.astype(jnp.bfloat16)).astype(jnp.float32)
        scale_rows = jnp.where(chosen[order], weight_row[order], jnp.float32(0.0))
        totals = totals.at[order].add(out_rows * scale_rows[:, None])
        return totals, None

    start_sums = jnp.zeros((TOKENS, D), jnp.float32)
    totals, ignored = lax.scan(expert_step, start_sums, jnp.arange(EXPERTS, dtype=jnp.int32))
    return totals.astype(jnp.bfloat16)
```

```python
import functools

import jax
import jax.numpy as jnp
from jax import lax
from jax.experimental import pallas as pl
from jax.experimental.pallas import tpu as pltpu
from jax.sharding import PartitionSpec as P

CAP = 16
PAIR = 2
HOP = 2
TERMS = 2
MESH = pl.DeviceIdType.MESH


def routes(nt):
    own, relay = [[] for _ in range(nt)], [[] for _ in range(nt)]
    for side in (-1, 1):
        end = nt - 1 if side > 0 else 0
        for s in range(nt):
            for dist in range(1, abs(end - s) + 1):
                to = s + side * dist
                back = 1 if to == end else dist - (dist - 1) // HOP * HOP
                holder = to - side * back
                if holder == s:
                    own[s].append(to)
                else:
                    relay[holder].append((s, to))
    for r in range(nt):
        own[r].sort(key=lambda to: -abs(to - r))
        relay[r].sort(key=lambda pair: abs(pair[0] - r))
    return own, relay


def kernel(
    nd, ne, nt,
    hidden_hbm, ids_hbm, weights_hbm, gate_hbm, up_hbm, down_hbm, out_ref,
    tokens_in, ids_ref, weights_ref, packed, feats, acts, gate_w, up_w, down_w,
    gate_acc, up_acc, down_acc, outgoing, returned, table, total,
    in_sem, w_sem, z_send, z_recv, f_send, f_recv, u_send, u_recv,
    ret_send, ret_recv,
):
    d, e, t = lax.axis_index("dp"), lax.axis_index("expert"), lax.axis_index("tensor")
    tokens, width = tokens_in.shape[1:]
    slots = ne * CAP
    units = gate_w.shape[2]
    nx = ne // PAIR
    groups = nd * nx
    rows = PAIR * CAP
    own, relay = routes(nt)

    def pick(values):
        value = values[0]
        for i in range(1, nt):
            value = jnp.where(t == i, values[i], value)
        return value

    order = [sorted(range(nt), key=lambda s: (abs(s - i), s)) for i in range(nt)]
    shard = [pick([order[i][k] for i in range(nt)]) for k in range(nt)]
    relayed = [
        pick([int(any(s == order[i][k] for s, _ in relay[i])) for i in range(nt)])
        for k in range(nt)
    ]

    def group(g):
        j, k = g // nx, lax.rem(g, nx)
        b = lax.rem(d + j, nd)
        base = pl.multiple_of(lax.rem(e // PAIR + k, nx) * PAIR, PAIR)
        return b, base

    barrier = pltpu.get_barrier_semaphore()
    for j in range(nd):
        for k in range(ne):
            if j or k:
                pl.semaphore_signal(
                    barrier, inc=1, device_id_type=MESH,
                    device_id=(lax.rem(d + j, nd), lax.rem(e + k, ne), t),
                )
    greeted = nd * ne - 1
    for k in range(-HOP, HOP + 1):
        if k:
            near = (t + k >= 0) & (t + k < nt)
            greeted += near.astype(jnp.int32)

            @pl.when(near)
            def _():
                pl.semaphore_signal(
                    barrier, inc=1, device_id=(d, e, t + k), device_id_type=MESH
                )
    inputs = (
        pltpu.make_async_copy(hidden_hbm, tokens_in.at[t], in_sem.at[2]),
        pltpu.make_async_copy(ids_hbm, ids_ref, in_sem.at[0]),
        pltpu.make_async_copy(weights_hbm, weights_ref, in_sem.at[1]),
    )
    for copy in inputs:
        copy.start()
    for copy in inputs:
        copy.wait()

    def weight_copy(i, s):
        size = units if i == 2 else width
        source = (gate_hbm, up_hbm, down_hbm)[i]
        return pltpu.make_async_copy(
            source.at[0, pl.ds(pl.multiple_of(s * size, size), size)],
            (gate_w, up_w, down_w)[i].at[s],
            w_sem.at[i, s],
        )

    for k in range(nt):
        weight_copy(0, shard[k]).start()
        weight_copy(1, shard[k]).start()
    for k in range(nt):
        weight_copy(2, shard[k]).start()

    slot = lax.broadcasted_iota(jnp.int32, (slots, tokens), 0)
    slot_expert = lax.shift_right_logical(slot, CAP.bit_length() - 1)
    slot_place = slot - slot_expert * CAP
    named = jnp.zeros((slots, tokens), jnp.float32)
    weighted = jnp.zeros((slots, tokens), jnp.float32)
    for row in range(ids_ref.shape[0]):
        match = ids_ref[row : row + 1, :] == slot_expert
        named = jnp.where(match, 1.0, named)
        weighted = jnp.where(match, weights_ref[row : row + 1, :], weighted)
    earlier = lax.broadcasted_iota(jnp.int32, (tokens, tokens), 0) < (
        lax.broadcasted_iota(jnp.int32, (tokens, tokens), 1)
    )
    position = jnp.dot(
        named.astype(jnp.bfloat16),
        jnp.where(earlier, 1.0, 0.0).astype(jnp.bfloat16),
        preferred_element_type=jnp.float32,
    )
    placing = jnp.where(position == slot_place.astype(jnp.float32), named, 0.0)
    rest = weighted * placing
    for i in range(TERMS):
        term = rest.astype(jnp.bfloat16)
        table[i] = term
        rest = rest - term.astype(jnp.float32)
    table[TERMS] = placing.astype(jnp.bfloat16)

    def z_copy(s, to):
        return pltpu.make_async_remote_copy(
            src_ref=tokens_in.at[s],
            dst_ref=tokens_in.at[s],
            send_sem=z_send.at[s, to],
            recv_sem=z_recv.at[s],
            device_id=(d, e, to),
            device_id_type=MESH,
        )

    def per_place(act):
        for i in range(nt):
            @pl.when(t == i)
            def _():
                act(i)

    def z_own(i):
        for to in own[i]:
            z_copy(i, to).start()

    def z_pass(k):
        def act(i):
            for s, to in relay[i]:
                if s == order[i][k]:
                    z_copy(s, to).start()

        per_place(act)

    def z_drain(i):
        for to in own[i]:
            z_copy(i, to).wait_send()
        for s, to in relay[i]:
            z_copy(s, to).wait_send()

    def f_copy(s, j, k):
        chip = lax.rem(e // PAIR + k // PAIR, nx)
        to = chip * PAIR + lax.rem(e + k, PAIR)
        return pltpu.make_async_remote_copy(
            src_ref=packed.at[s, to],
            dst_ref=feats.at[d, s, e],
            send_sem=f_send.at[j, s, k],
            recv_sem=f_recv.at[d, s, e],
            device_id=(lax.rem(d + j, nd), to, t),
            device_id_type=MESH,
        )

    def f_wait(b, s, source):
        pltpu.make_async_remote_copy(
            src_ref=packed.at[s, source],
            dst_ref=feats.at[b, s, source],
            send_sem=f_send.at[0, s, 0],
            recv_sem=f_recv.at[b, s, source],
            device_id=(b, source, t),
            device_id_type=MESH,
        ).wait_recv()

    def spread(s):
        packed[s] = (
            jnp.dot(table[TERMS], tokens_in[s], preferred_element_type=jnp.float32)
            .astype(jnp.bfloat16)
            .reshape(ne, CAP, width)
        )
        for k in range(1, ne):
            f_copy(s, 0, k).start()
        for j in range(1, nd):
            for k in range(PAIR):
                f_copy(s, j, k).start()
        feats[d, s, e] = packed[s, e]

    def spread_far(s):
        for j in range(1, nd):
            for k in range(PAIR, ne):
                f_copy(s, j, k).start()

    def f_arrive(g, s):
        b, base = group(g)
        for c in range(PAIR):
            @pl.when((b != d) | (base + c != e))
            def _():
                f_wait(b, s, base + c)

    def gate_up(g, k):
        b, base = group(g)
        s = shard[k]
        x = feats[b, s, pl.ds(base, PAIR)].reshape(rows, width)
        gate = jnp.dot(x, gate_w[s], preferred_element_type=jnp.float32)
        up = jnp.dot(x, up_w[s], preferred_element_type=jnp.float32)
        if k == 0:
            gate_acc[...] = gate
            up_acc[...] = up
        else:
            gate_acc[...] += gate
            up_acc[...] += up

    def activate(g):
        b, base = group(g)
        gate = gate_acc[...]
        value = gate / (1.0 + jnp.exp(-gate)) * up_acc[...]
        acts[b, t, pl.ds(base, PAIR)] = value.astype(jnp.bfloat16).reshape(PAIR, CAP, units)

    def u_copy(g, s, to, send_sem):
        b, base = group(g)
        block = acts.at[b, s, pl.ds(base, PAIR)]
        return pltpu.make_async_remote_copy(
            src_ref=block,
            dst_ref=block,
            send_sem=send_sem,
            recv_sem=u_recv.at[g, s],
            device_id=(d, e, to),
            device_id_type=MESH,
        )

    def u_own(g):
        def act(i):
            for to in own[i]:
                u_copy(g, i, to, u_send.at[g, i, to]).start()

        per_place(act)

    def u_pass(g):
        def act(i):
            held = None
            for s, to in relay[i]:
                copy = u_copy(g, s, to, u_send.at[g, s, to])
                if s != held:
                    copy.wait_recv()
                held = s
                copy.start()

        per_place(act)

    def u_drain(g):
        def act(i):
            for s, to in [(i, to) for to in own[i]] + relay[i]:
                u_copy(g, s, to, u_send.at[g, s, to]).wait_send()

        per_place(act)

    def down(g, k):
        b, base = group(g)
        s = shard[k]
        h = acts[b, s, pl.ds(base, PAIR)].reshape(rows, units)
        value = jnp.dot(h, down_w[s], preferred_element_type=jnp.float32)
        if k == 0:
            down_acc[...] = value
        else:
            down_acc[...] += value

    def ret_copy(g, c):
        b, base = group(g)
        return pltpu.make_async_remote_copy(
            src_ref=outgoing.at[b, base + c],
            dst_ref=returned.at[d, e],
            send_sem=ret_send.at[g, c],
            recv_sem=ret_recv.at[d, e],
            device_id=(b, base + c, t),
            device_id_type=MESH,
        )

    def ret_each(g, act, local):
        b, base = group(g)
        for c in range(PAIR):
            here = (b == d) & (base + c == e)

            @pl.when(jnp.logical_not(here))
            def _():
                act(c)

            if local is not None:
                @pl.when(here)
                def _():
                    local()

    def ret_wait(g, c):
        b, base = group(g)
        pltpu.make_async_remote_copy(
            src_ref=outgoing.at[0, 0],
            dst_ref=returned.at[b, base + c],
            send_sem=ret_send.at[g, c],
            recv_sem=ret_recv.at[b, base + c],
            device_id=(b, base + c, t),
            device_id_type=MESH,
        ).wait_recv()

    with jax.named_scope("barrier"):
        pl.semaphore_wait(barrier, greeted)
    per_place(z_own)
    spread(t)
    for k in range(nt):
        if k + 1 < nt:
            s = shard[k + 1]
            with jax.named_scope("z_arrive"):
                pltpu.make_async_remote_copy(
                    src_ref=tokens_in.at[s], dst_ref=tokens_in.at[s],
                    send_sem=z_send.at[s, 0], recv_sem=z_recv.at[s],
                    device_id=(d, e, s), device_id_type=MESH,
                ).wait_recv()
                z_pass(k + 1)
            with jax.named_scope("spread"):
                spread(s)
        with jax.named_scope("f_arrive"):
            f_arrive(0, shard[k])
        with jax.named_scope("w_arrive"):
            weight_copy(0, shard[k]).wait()
            weight_copy(1, shard[k]).wait()
        with jax.named_scope("gate_up"):
            gate_up(0, k)
    with jax.named_scope("activate"):
        activate(0)
        u_own(0)
    for k in range(nt):
        spread_far(shard[k])

    def hidden(g, carry):
        for k in range(nt):
            with jax.named_scope("f_arrive"):
                f_arrive(g, shard[k])
            with jax.named_scope("gate_up"):
                gate_up(g, k)
            if k == nt - 2:
                @pl.when(g > 1)
                def _():
                    with jax.named_scope("forward"):
                        u_pass(g - 2)
        with jax.named_scope("activate"):
            activate(g)
            u_own(g)
        return carry

    lax.fori_loop(1, groups, hidden, 0)

    with jax.named_scope("forward"):
        for g in range(max(groups - 2, 0), groups - 1):
            u_pass(g)
    for k in range(nt):
        weight_copy(2, shard[k]).wait()

    def finish(g, carry):
        for k in range(nt):
            if k:
                with jax.named_scope("u_arrive"):
                    @pl.when(relayed[k] == 0)
                    def _():
                        u_copy(g, shard[k], t, u_send.at[g, 0, 0]).wait_recv()
            with jax.named_scope("down"):
                down(g, k)
        b, base = group(g)
        outgoing[b, pl.ds(base, PAIR)] = (
            down_acc[...].astype(jnp.bfloat16).reshape(PAIR, CAP, width)
        )

        def keep():
            returned[d, e] = outgoing[d, e]

        ret_each(g, lambda c: ret_copy(g, c).start(), keep)

        @pl.when(g == 0)
        def _():
            with jax.named_scope("forward"):
                u_pass(groups - 1)

        return carry

    lax.fori_loop(0, groups, finish, 0)

    total[...] = jnp.zeros((tokens, width), jnp.float32)

    def combine(g, carry):
        with jax.named_scope("ret_arrive"):
            ret_each(g, lambda c: ret_wait(g, c), None)
        with jax.named_scope("combine"):
            b, base = group(g)
            back = returned[b, pl.ds(base, PAIR)].reshape(rows, width)
            places = pl.ds(pl.multiple_of(base * CAP, rows), rows)
            for i in range(TERMS):
                total[...] += lax.dot_general(
                    table[i, places], back, (((0,), (0,)), ((), ())),
                    preferred_element_type=jnp.float32,
                )
        return carry

    lax.fori_loop(0, groups, combine, 0)
    out_ref[...] = total[...].astype(jnp.bfloat16)

    with jax.named_scope("drain"):
        per_place(z_drain)
        for s in range(nt):
            for j in range(nd):
                for k in range(ne):
                    if j or k:
                        f_copy(s, j, k).wait_send()

        def drain(g, carry):
            u_drain(g)
            ret_each(g, lambda c: ret_copy(g, c).wait_send(), None)
            return carry

        lax.fori_loop(0, groups, drain, 0)


def body(mesh, hidden_states, chosen_experts, choice_weights, gate_proj, up_proj, down_proj):
    nd, ne, nt = mesh.shape["dp"], mesh.shape["expert"], mesh.shape["tensor"]
    tokens, width = hidden_states.shape
    units = gate_proj.shape[2]
    slots = ne * CAP
    rows = PAIR * CAP
    groups = nd * ne // PAIR
    vmem = pl.BlockSpec(memory_space=pltpu.VMEM)
    hbm = pl.BlockSpec(memory_space=pltpu.HBM)
    bf16, f32, dma = jnp.bfloat16, jnp.float32, pltpu.SemaphoreType.DMA
    operands = [
        pltpu.with_memory_space_constraint(x, pltpu.HBM)
        for x in (hidden_states, chosen_experts.T, choice_weights.T, gate_proj, up_proj, down_proj)
    ]
    return pl.pallas_call(
        functools.partial(kernel, nd, ne, nt),
        out_shape=jax.ShapeDtypeStruct((tokens, width), bf16),
        in_specs=[hbm] * 6,
        out_specs=vmem,
        scratch_shapes=[
            pltpu.VMEM((nt, tokens, width), bf16),
            pltpu.VMEM(chosen_experts.shape[::-1], jnp.int32),
            pltpu.VMEM(choice_weights.shape[::-1], f32),
            pltpu.VMEM((nt, ne, CAP, width), bf16),
            pltpu.VMEM((nd, nt, ne, CAP, width), bf16),
            pltpu.VMEM((nd, nt, ne, CAP, units), bf16),
            pltpu.VMEM((nt, width, units), bf16),
            pltpu.VMEM((nt, width, units), bf16),
            pltpu.VMEM((nt, units, width), bf16),
            pltpu.VMEM((rows, units), f32),
            pltpu.VMEM((rows, units), f32),
            pltpu.VMEM((rows, width), f32),
            pltpu.VMEM((nd, ne, CAP, width), bf16),
            pltpu.VMEM((nd, ne, CAP, width), bf16),
            pltpu.VMEM((TERMS + 1, slots, tokens), bf16),
            pltpu.VMEM((tokens, width), f32),
            dma((3,)),
            dma((3, nt)),
            dma((nt, nt)),
            dma((nt,)),
            dma((nd, nt, ne)),
            dma((nd, nt, ne)),
            dma((groups, nt, nt)),
            dma((groups, nt)),
            dma((groups, PAIR)),
            dma((nd, ne)),
        ],
        compiler_params=pltpu.CompilerParams(
            collective_id=0, has_side_effects=True, vmem_limit_bytes=48 << 20
        ),
        name="experts",
    )(*operands)


def solution(mesh):
    in_specs = (
        P(("dp", "expert"), "tensor"),
        P(("dp", "expert"), None),
        P(("dp", "expert"), None),
        P("expert", None, ("dp", "tensor")),
        P("expert", None, ("dp", "tensor")),
        P("expert", "dp", "tensor"),
    )
    out_specs = P(("dp", "expert"), "tensor")
    return jax.shard_map(
        functools.partial(body, mesh), mesh=mesh, in_specs=in_specs, out_specs=out_specs,
        check_vma=False,
    )
```

```python
import functools

import jax
import jax.numpy as jnp
from jax import lax
from jax.experimental import pallas as pl
from jax.experimental.pallas import tpu as pltpu
from jax.sharding import PartitionSpec as P

CAP = 16
PAIR = 2
HOP = 2
TERMS = 2
MESH = pl.DeviceIdType.MESH


def routes(nt):
    own, relay = [[] for _ in range(nt)], [[] for _ in range(nt)]
    for side in (-1, 1):
        end = nt - 1 if side > 0 else 0
        for s in range(nt):
            for dist in range(1, abs(end - s) + 1):
                to = s + side * dist
                back = 1 if to == end else dist - (dist - 1) // HOP * HOP
                holder = to - side * back
                if holder == s:
                    own[s].append(to)
                else:
                    relay[holder].append((s, to))
    for r in range(nt):
        own[r].sort(key=lambda to: -abs(to - r))
        relay[r].sort(key=lambda pair: abs(pair[0] - r))
    return own, relay


def kernel(
    nd, ne, nt,
    hidden_hbm, ids_hbm, weights_hbm, gate_hbm, up_hbm, down_hbm, out_ref,
    tokens_in, ids_ref, weights_ref, packed, feats, acts, gate_up_w, down_w,
    gate_acc, up_acc, down_acc, outgoing, returned, table, total,
    in_sem, w_sem, z_send, z_recv, f_send, f_recv, u_send, u_recv,
    ret_send, ret_recv,
):
    d, e, t = lax.axis_index("dp"), lax.axis_index("expert"), lax.axis_index("tensor")
    tokens, width = tokens_in.shape[1:]
    slots = ne * CAP
    units = gate_up_w.shape[3]
    parts = acts.shape[1]
    share = units // parts
    nx = ne // PAIR
    groups = nd * nx
    rows = PAIR * CAP
    own, relay = routes(nt)

    def pick(values):
        value = values[0]
        for i in range(1, nt):
            value = jnp.where(t == i, values[i], value)
        return value

    order = [
        sorted(range(nt), key=lambda s: (abs(s - i), abs(2 * s - nt + 1))) for i in range(nt)
    ]
    shard = [pick([order[i][k] for i in range(nt)]) for k in range(nt)]
    passed = [
        pick([int(any(s == order[i][k] for s, _ in relay[i])) for i in range(nt)])
        for k in range(nt)
    ]
    batches = 1 + groups // 2

    def of_batch(index, act):
        if isinstance(index, int):
            return act(tuple(range(max(2 * index - 1, 0), min(2 * index + 1, groups))))

        @pl.when(index == 0)
        def _():
            act((0,))

        if batches > 2 - groups % 2:
            @pl.when((index > 0) & (2 * index < groups))
            def _():
                act((2 * index - 1, 2 * index))

        if groups % 2 == 0:
            @pl.when(index == batches - 1)
            def _():
                act((groups - 1,))

    def group(g):
        j, k = g // nx, lax.rem(g, nx)
        b = lax.rem(d + j, nd)
        base = pl.multiple_of(lax.rem(e // PAIR + k, nx) * PAIR, PAIR)
        return b, base

    barrier = pltpu.get_barrier_semaphore()
    for j in range(nd):
        for k in range(ne):
            if j or k:
                pl.semaphore_signal(
                    barrier, inc=1, device_id_type=MESH,
                    device_id=(lax.rem(d + j, nd), lax.rem(e + k, ne), t),
                )
    greeted = nd * ne - 1
    for k in range(-HOP, HOP + 1):
        if k:
            near = (t + k >= 0) & (t + k < nt)
            greeted += near.astype(jnp.int32)

            @pl.when(near)
            def _():
                pl.semaphore_signal(
                    barrier, inc=1, device_id=(d, e, t + k), device_id_type=MESH
                )
    inputs = (
        pltpu.make_async_copy(hidden_hbm, tokens_in.at[t], in_sem.at[2]),
        pltpu.make_async_copy(ids_hbm, ids_ref, in_sem.at[0]),
        pltpu.make_async_copy(weights_hbm, weights_ref, in_sem.at[1]),
    )
    for copy in inputs:
        copy.start()

    def gate_up_copy(i, s):
        return pltpu.make_async_copy(
            (gate_hbm, up_hbm)[i].at[0, pl.ds(pl.multiple_of(s * width, width), width)],
            gate_up_w.at[s, i],
            w_sem.at[s],
        )

    def down_copy(s):
        return pltpu.make_async_copy(
            down_hbm.at[0, pl.ds(pl.multiple_of(s * units, units), units)],
            down_w.at[s],
            w_sem.at[nt],
        )

    gate_up_copy(0, t).start()
    gate_up_copy(1, t).start()

    def per_place(act):
        for i in range(nt):
            @pl.when(t == i)
            def _():
                act(i)

    def z_copy(s, to, sem, source=None):
        return pltpu.make_async_remote_copy(
            src_ref=tokens_in.at[s] if source is None else source,
            dst_ref=tokens_in.at[s],
            send_sem=z_send.at[sem],
            recv_sem=z_recv.at[s],
            device_id=(d, e, to),
            device_id_type=MESH,
        )

    def z_own(i):
        for to in own[i]:
            z_copy(i, to, 0, hidden_hbm).start()

    with jax.named_scope("barrier"):
        pl.semaphore_wait(barrier, greeted)
    per_place(z_own)
    for copy in inputs:
        copy.wait()
    for k in range(1, nt):
        gate_up_copy(0, shard[k]).start()
        gate_up_copy(1, shard[k]).start()
    for k in range(nt):
        down_copy(shard[k]).start()

    slot = lax.broadcasted_iota(jnp.int32, (slots, tokens), 0)
    slot_expert = lax.shift_right_logical(slot, CAP.bit_length() - 1)
    slot_place = slot - slot_expert * CAP
    named = jnp.zeros((slots, tokens), jnp.float32)
    weighted = jnp.zeros((slots, tokens), jnp.float32)
    for row in range(ids_ref.shape[0]):
        match = ids_ref[row : row + 1, :] == slot_expert
        named = jnp.where(match, 1.0, named)
        weighted = jnp.where(match, weights_ref[row : row + 1, :], weighted)
    earlier = lax.broadcasted_iota(jnp.int32, (tokens, tokens), 0) < (
        lax.broadcasted_iota(jnp.int32, (tokens, tokens), 1)
    )
    position = jnp.dot(
        named.astype(jnp.bfloat16),
        jnp.where(earlier, 1.0, 0.0).astype(jnp.bfloat16),
        preferred_element_type=jnp.float32,
    )
    placing = jnp.where(position == slot_place.astype(jnp.float32), named, 0.0)
    rest = weighted * placing
    for i in range(TERMS):
        term = rest.astype(jnp.bfloat16)
        table[i] = term
        rest = rest - term.astype(jnp.float32)
    table[TERMS] = placing.astype(jnp.bfloat16)

    def sent(ref, count, sem):
        if count:
            part = ref.at[pl.ds(0, count)]
            pltpu.make_async_copy(part, part, sem).wait()

    def z_wait(s):
        z_copy(s, t, 0).wait_recv()

    def z_pass(i):
        held = order[i][1]
        for s, to in relay[i]:
            if s != held:
                z_wait(s)
            held = s
            z_copy(s, to, 1).start()

    def z_drain(i):
        sent(tokens_in, len(own[i]), z_send.at[0])
        sent(tokens_in, len(relay[i]), z_send.at[1])

    def place(b, s, source):
        return (b * nt + s) * ne + source

    def f_copy(s, j, k):
        chip = lax.rem(e // PAIR + k // PAIR, nx)
        to = chip * PAIR + lax.rem(e + k, PAIR)
        return pltpu.make_async_remote_copy(
            src_ref=packed.at[s, to],
            dst_ref=feats.at[place(d, s, e)],
            send_sem=f_send.at[0],
            recv_sem=f_recv.at[d, s, e // PAIR],
            device_id=(lax.rem(d + j, nd), to, t),
            device_id_type=MESH,
        )

    def spread(s):
        packed[s] = (
            jnp.dot(table[TERMS], tokens_in[s], preferred_element_type=jnp.float32)
            .astype(jnp.bfloat16)
            .reshape(ne, CAP, width)
        )
        for k in range(1, ne):
            f_copy(s, 0, k).start()
        for j in range(1, nd):
            for k in range(PAIR):
                f_copy(s, j, k).start()
        feats[place(d, s, e)] = packed[s, e]

    def spread_far(s):
        for j in range(1, nd):
            for k in range(PAIR, ne):
                f_copy(s, j, k).start()

    def f_arrive(g, s):
        b, base = group(g)
        count = PAIR - 1 if isinstance(g, int) and g == 0 else PAIR
        block = feats.at[pl.ds(place(b, s, base), count)]
        pltpu.make_async_copy(block, block, f_recv.at[b, s, base // PAIR]).wait()

    def gate_up(gs, k, p=None):
        s = shard[k]
        columns = slice(None) if p is None else slice(p * share, (p + 1) * share)
        x = [
            feats[pl.ds(place(b, s, base), PAIR)].reshape(rows, width)
            for b, base in map(group, gs)
        ]
        x = jnp.concatenate(x) if len(gs) > 1 else x[0]
        here = slice(0, rows * len(gs))
        gate = jnp.dot(x, gate_up_w[s, 0, :, columns], preferred_element_type=jnp.float32)
        up = jnp.dot(x, gate_up_w[s, 1, :, columns], preferred_element_type=jnp.float32)
        if k == 0:
            gate_acc[here, columns] = gate
            up_acc[here, columns] = up
        else:
            gate_acc[here, columns] += gate
            up_acc[here, columns] += up

    def unit_place(b, s, base):
        return (b * nt + s) * nx + base // PAIR

    def activate(gs, p):
        for i, g in enumerate(gs):
            b, base = group(g)
            here, columns = pl.ds(i * rows, rows), pl.ds(p * share, share)
            gate = gate_acc[here, columns]
            value = gate / (1.0 + jnp.exp(-gate)) * up_acc[here, columns]
            acts[unit_place(b, t, base), p] = value.astype(jnp.bfloat16)
            u_own(g, p)

    def u_copy(g, s, to, sem, p=None):
        b, base = group(g)
        block = acts.at[unit_place(b, s, base)]
        if p is not None:
            block = block.at[p]
        return pltpu.make_async_remote_copy(
            src_ref=block,
            dst_ref=block,
            send_sem=u_send.at[sem],
            recv_sem=u_recv.at[g, s],
            device_id=(d, e, to),
            device_id_type=MESH,
        )

    def patient(i):
        return [to for to in own[i] if i in (0, nt - 1) and abs(to - i) == 1 and len(own[i]) > 1]

    def u_own(g, p):
        def act(i):
            for to in own[i]:
                if to not in patient(i):
                    u_copy(g, i, to, 0, p).start()

        per_place(act)

    def u_late(gs):
        def act(i):
            for g in gs:
                for to in patient(i):
                    u_copy(g, i, to, 0).start()

        per_place(act)

    def u_pass(gs, near):
        def act(i):
            for g in gs:
                held = None
                for s, to in relay[i]:
                    if (abs(s - i) == 1) == near:
                        copy = u_copy(g, s, to, 1)
                        if s != held:
                            copy.wait_recv()
                        held = s
                        copy.start()

        with jax.named_scope("pass_near" if near else "pass_far"):
            per_place(act)

    def u_take(g, k):
        @pl.when(passed[k] == 0)
        def _():
            u_copy(g, shard[k], t, 0).wait_recv()

    def u_drain(i):
        sent(acts, groups * len(own[i]), u_send.at[0])
        sent(acts, groups * len(relay[i]), u_send.at[1])

    def down(gs, k):
        s = shard[k]
        h = [
            jnp.concatenate([acts[unit_place(b, s, base), p] for p in range(parts)], axis=1)
            for b, base in map(group, gs)
        ]
        h = jnp.concatenate(h) if len(gs) > 1 else h[0]
        value = jnp.dot(h, down_w[s], preferred_element_type=jnp.float32)
        for i, g in enumerate(gs):
            part = value[i * rows : (i + 1) * rows]
            if k == 0:
                down_acc[g] = part
            else:
                down_acc[g] += part

    def ret_copy(g, c):
        b, base = group(g)
        return pltpu.make_async_remote_copy(
            src_ref=outgoing.at[b * ne + base + c],
            dst_ref=returned.at[d * ne + e],
            send_sem=ret_send.at[0],
            recv_sem=ret_recv.at[d, e // PAIR],
            device_id=(b, base + c, t),
            device_id_type=MESH,
        )

    def give_back(g):
        b, base = group(g)
        first = pl.multiple_of(b * ne + base, PAIR)
        outgoing[pl.ds(first, PAIR)] = (
            down_acc[g].astype(jnp.bfloat16).reshape(PAIR, CAP, width)
        )
        for c in range(PAIR):
            here = (b == d) & (base + c == e)

            @pl.when(jnp.logical_not(here))
            def _():
                ret_copy(g, c).start()

            @pl.when(here)
            def _():
                returned[d * ne + e] = outgoing[d * ne + e]

    def ret_arrive(g, count):
        b, base = group(g)
        block = returned.at[pl.ds(b * ne + base, count)]
        pltpu.make_async_copy(block, block, ret_recv.at[b, base // PAIR]).wait()

    spread(t)
    spread_far(t)

    def first_batch(k):
        with jax.named_scope("f_arrive"):
            f_arrive(0, shard[k])
        with jax.named_scope("w_arrive"):
            pltpu.make_async_copy(
                gate_up_w.at[shard[k]], gate_up_w.at[shard[k]], w_sem.at[shard[k]]
            ).wait()
        for p in range(parts) if k == nt - 1 else (None,):
            with jax.named_scope("gate_up"):
                gate_up((0,), k, p)
            if p is not None:
                with jax.named_scope("activate"):
                    activate((0,), p)

    first_batch(0)
    busy = functools.reduce(jnp.logical_or, [t == i for i in range(nt) if relay[i]], t < 0)
    with jax.named_scope("z_arrive"):
        z_wait(shard[1])
        per_place(z_pass)
    with jax.named_scope("spread"):
        spread(shard[1])

    @pl.when(jnp.logical_not(busy))
    def _():
        first_batch(1)

    for k in range(2, nt):
        with jax.named_scope("z_arrive"):
            @pl.when(passed[k] == 0)
            def _():
                z_wait(shard[k])
        with jax.named_scope("spread"):
            spread(shard[k])

    @pl.when(busy)
    def _():
        first_batch(1)

    for k in range(2, nt):
        first_batch(k)
    for k in range(1, nt):
        spread_far(shard[k])

    def later_batch(index, gs):
        for p in range(parts):
            for k in range(nt):
                if p == 0:
                    with jax.named_scope("f_arrive"):
                        for g in gs:
                            f_arrive(g, shard[k])
                with jax.named_scope("gate_up"):
                    gate_up(gs, k, p)
                if p == 0 and k == nt - 2:
                    @pl.when(index == 2)
                    def _():
                        u_pass((0,), False)

                    @pl.when(index > 2)
                    def _():
                        of_batch(index - 2, lambda old: u_pass(old, True))
            with jax.named_scope("activate"):
                activate(gs, p)
        of_batch(index - 1, u_late)

        @pl.when(index == 1)
        def _():
            u_pass((0,), True)

        @pl.when(index > 1)
        def _():
            of_batch(index - 1, lambda old: u_pass(old, False))

    def pair_batch(index, carry):
        later_batch(index, (2 * index - 1, 2 * index))
        return carry

    lax.fori_loop(1, (groups + 1) // 2, pair_batch, 0)
    if groups % 2 == 0:
        later_batch(batches - 1, (groups - 1,))
    of_batch(batches - 1, u_late)

    pltpu.make_async_copy(down_w, down_w, w_sem.at[nt]).wait()

    def finish(q, carry):
        if batches > 1:
            @pl.when(q == 2)
            def _():
                of_batch(batches - 2, lambda gs: u_pass(gs, batches > 2))

        @pl.when(q == min(3, batches))
        def _():
            of_batch(batches - 1, lambda gs: u_pass(gs, True))

        @pl.when(q == min(3, batches))
        def _():
            of_batch(batches - 1, lambda gs: u_pass(gs, False))

        def step(k, gs):
            if k:
                with jax.named_scope("u_arrive%d" % k):
                    for g in gs:
                        u_take(g, k)
            with jax.named_scope("down"):
                down(gs, k)
            if k == nt - 1:
                for g in gs:
                    give_back(g)

        for k in range(nt):
            @pl.when((q >= k) & (q - k < batches))
            def _():
                of_batch(q - k, functools.partial(step, k))

        return carry

    lax.fori_loop(0, batches + nt - 1, finish, 0)

    total[...] = jnp.zeros((tokens, width), jnp.float32)

    def combine(g):
        with jax.named_scope("ret_arrive"):
            ret_arrive(g, PAIR - 1 if isinstance(g, int) else PAIR)
        with jax.named_scope("combine"):
            b, base = group(g)
            back = returned[pl.ds(b * ne + base, PAIR)].reshape(rows, width)
            places = pl.ds(pl.multiple_of(base * CAP, rows), rows)
            for i in range(TERMS):
                total[...] += lax.dot_general(
                    table[i, places], back, (((0,), (0,)), ((), ())),
                    preferred_element_type=jnp.float32,
                )

    combine(0)
    lax.fori_loop(1, groups, lambda g, carry: (combine(g), carry)[1], 0)
    out_ref[...] = total[...].astype(jnp.bfloat16)

    with jax.named_scope("drain"):
        per_place(z_drain)
        sent(feats, nt * (nd * ne - 1), f_send.at[0])
        per_place(u_drain)
        sent(outgoing, nd * ne - 1, ret_send.at[0])


def body(mesh, hidden_states, chosen_experts, choice_weights, gate_proj, up_proj, down_proj):
    nd, ne, nt = mesh.shape["dp"], mesh.shape["expert"], mesh.shape["tensor"]
    tokens, width = hidden_states.shape
    units = gate_proj.shape[2]
    slots = ne * CAP
    rows = PAIR * CAP
    groups = nd * ne // PAIR
    parts = 1 if units % 256 else 2
    vmem = pl.BlockSpec(memory_space=pltpu.VMEM)
    hbm = pl.BlockSpec(memory_space=pltpu.HBM)
    bf16, f32, dma = jnp.bfloat16, jnp.float32, pltpu.SemaphoreType.DMA
    operands = [
        pltpu.with_memory_space_constraint(x, pltpu.HBM)
        for x in (hidden_states, chosen_experts.T, choice_weights.T, gate_proj, up_proj, down_proj)
    ]
    return pl.pallas_call(
        functools.partial(kernel, nd, ne, nt),
        out_shape=jax.ShapeDtypeStruct((tokens, width), bf16),
        in_specs=[hbm] * 6,
        out_specs=vmem,
        scratch_shapes=[
            pltpu.VMEM((nt, tokens, width), bf16),
            pltpu.VMEM(chosen_experts.shape[::-1], jnp.int32),
            pltpu.VMEM(choice_weights.shape[::-1], f32),
            pltpu.VMEM((nt, ne, CAP, width), bf16),
            pltpu.VMEM((nd * nt * ne, CAP, width), bf16),
            pltpu.VMEM((groups * nt, parts, rows, units // parts), bf16),
            pltpu.VMEM((nt, 2, width, units), bf16),
            pltpu.VMEM((nt, units, width), bf16),
            pltpu.VMEM((2 * rows, units), f32),
            pltpu.VMEM((2 * rows, units), f32),
            pltpu.VMEM((groups, rows, width), f32),
            pltpu.VMEM((nd * ne, CAP, width), bf16),
            pltpu.VMEM((nd * ne, CAP, width), bf16),
            pltpu.VMEM((TERMS + 1, slots, tokens), bf16),
            pltpu.VMEM((tokens, width), f32),
            dma((3,)),
            dma((nt + 1,)),
            dma((2,)),
            dma((nt,)),
            dma((1,)),
            dma((nd, nt, ne // PAIR)),
            dma((2,)),
            dma((groups, nt)),
            dma((1,)),
            dma((nd, ne // PAIR)),
        ],
        compiler_params=pltpu.CompilerParams(
            collective_id=0, has_side_effects=True, vmem_limit_bytes=48 << 20
        ),
        name="experts",
    )(*operands)


def solution(mesh):
    in_specs = (
        P(("dp", "expert"), "tensor"),
        P(("dp", "expert"), None),
        P(("dp", "expert"), None),
        P("expert", None, ("dp", "tensor")),
        P("expert", None, ("dp", "tensor")),
        P("expert", "dp", "tensor"),
    )
    out_specs = P(("dp", "expert"), "tensor")
    return jax.shard_map(
        functools.partial(body, mesh), mesh=mesh, in_specs=in_specs, out_specs=out_specs,
        check_vma=False,
    )
```

```python
import functools

import jax
import jax.numpy as jnp
from jax import lax
from jax.experimental import pallas as pl
from jax.experimental.pallas import tpu as pltpu
from jax.sharding import PartitionSpec as P

CAP = 16
PAIR = 2
HOP = 2
TERMS = 2
MESH = pl.DeviceIdType.MESH


def routes(nt):
    own, relay = [[] for _ in range(nt)], [[] for _ in range(nt)]
    for side in (-1, 1):
        end = nt - 1 if side > 0 else 0
        for s in range(nt):
            for dist in range(1, abs(end - s) + 1):
                to = s + side * dist
                back = 1 if to == end else dist - (dist - 1) // HOP * HOP
                holder = to - side * back
                if holder == s:
                    own[s].append(to)
                else:
                    relay[holder].append((s, to))
    for r in range(nt):
        own[r].sort(key=lambda to: -abs(to - r))
        relay[r].sort(key=lambda pair: abs(pair[0] - r))
    return own, relay


def kernel(
    nd, ne, nt,
    hidden_hbm, ids_hbm, weights_hbm, gate_hbm, up_hbm, down_hbm, out_ref,
    tokens_in, ids_ref, weights_ref, packed, feats, acts, gate_up_w, down_w,
    gate_acc, up_acc, down_acc, outgoing, returned, table, total,
    in_sem, w_sem, z_send, z_recv, f_send, f_recv, u_send, u_recv,
    ret_send, ret_recv,
):
    d, e, t = lax.axis_index("dp"), lax.axis_index("expert"), lax.axis_index("tensor")
    tokens, width = tokens_in.shape[1:]
    slots = ne * CAP
    units = gate_up_w.shape[3]
    parts = acts.shape[1]
    share = units // parts
    nx = ne // PAIR
    groups = nd * nx
    rows = PAIR * CAP
    own, relay = routes(nt)

    def pick(values):
        value = values[0]
        for i in range(1, nt):
            value = jnp.where(t == i, values[i], value)
        return value

    order = [
        sorted(range(nt), key=lambda s: (abs(s - i), abs(2 * s - nt + 1))) for i in range(nt)
    ]
    shard = [pick([order[i][k] for i in range(nt)]) for k in range(nt)]
    passed = [
        pick([int(any(s == order[i][k] for s, _ in relay[i])) for i in range(nt)])
        for k in range(nt)
    ]
    batches = 1 + groups // 2
    listed = nt == 4 and groups == 4
    far_corner = (d == nd - 1) & (e // PAIR == nx - 1)
    at_end = (t == 0) | (t == nt - 1)

    def of_batch(index, act):
        if isinstance(index, int):
            return act(tuple(range(max(2 * index - 1, 0), min(2 * index + 1, groups))))

        @pl.when(index == 0)
        def _():
            act((0,))

        if batches > 2 - groups % 2:
            @pl.when((index > 0) & (2 * index < groups))
            def _():
                act((2 * index - 1, 2 * index))

        if groups % 2 == 0:
            @pl.when(index == batches - 1)
            def _():
                act((groups - 1,))

    def group(g):
        j, k = g // nx, lax.rem(g, nx)
        b = lax.rem(d + j, nd)
        base = pl.multiple_of(lax.rem(e // PAIR + k, nx) * PAIR, PAIR)
        return b, base

    barrier = pltpu.get_barrier_semaphore()
    for j in range(nd):
        for k in range(ne):
            if j or k:
                pl.semaphore_signal(
                    barrier, inc=1, device_id_type=MESH,
                    device_id=(lax.rem(d + j, nd), lax.rem(e + k, ne), t),
                )
    greeted = nd * ne - 1
    for k in range(-HOP, HOP + 1):
        if k:
            near = (t + k >= 0) & (t + k < nt)
            greeted += near.astype(jnp.int32)

            @pl.when(near)
            def _():
                pl.semaphore_signal(
                    barrier, inc=1, device_id=(d, e, t + k), device_id_type=MESH
                )
    inputs = (
        pltpu.make_async_copy(hidden_hbm, tokens_in.at[t], in_sem.at[2]),
        pltpu.make_async_copy(ids_hbm, ids_ref, in_sem.at[0]),
        pltpu.make_async_copy(weights_hbm, weights_ref, in_sem.at[1]),
    )
    for copy in inputs:
        copy.start()

    def gate_up_copy(i, s):
        return pltpu.make_async_copy(
            (gate_hbm, up_hbm)[i].at[0, pl.ds(pl.multiple_of(s * width, width), width)],
            gate_up_w.at[s, i],
            w_sem.at[s],
        )

    def down_copy(s):
        return pltpu.make_async_copy(
            down_hbm.at[0, pl.ds(pl.multiple_of(s * units, units), units)],
            down_w.at[s],
            w_sem.at[nt],
        )

    gate_up_copy(0, t).start()
    gate_up_copy(1, t).start()

    def per_place(act):
        for i in range(nt):
            @pl.when(t == i)
            def _():
                act(i)

    def z_copy(s, to, sem, source=None):
        return pltpu.make_async_remote_copy(
            src_ref=tokens_in.at[s] if source is None else source,
            dst_ref=tokens_in.at[s],
            send_sem=z_send.at[sem],
            recv_sem=z_recv.at[s],
            device_id=(d, e, to),
            device_id_type=MESH,
        )

    def z_own(i):
        for to in own[i]:
            z_copy(i, to, 0, hidden_hbm).start()

    with jax.named_scope("barrier"):
        pl.semaphore_wait(barrier, greeted)
    per_place(z_own)
    for copy in inputs:
        copy.wait()
    for k in range(1, nt):
        gate_up_copy(0, shard[k]).start()
        gate_up_copy(1, shard[k]).start()
    for k in range(nt):
        down_copy(shard[k]).start()

    slot = lax.broadcasted_iota(jnp.int32, (slots, tokens), 0)
    slot_expert = lax.shift_right_logical(slot, CAP.bit_length() - 1)
    slot_place = slot - slot_expert * CAP
    named = jnp.zeros((slots, tokens), jnp.float32)
    weighted = jnp.zeros((slots, tokens), jnp.float32)
    for row in range(ids_ref.shape[0]):
        match = ids_ref[row : row + 1, :] == slot_expert
        named = jnp.where(match, 1.0, named)
        weighted = jnp.where(match, weights_ref[row : row + 1, :], weighted)
    earlier = lax.broadcasted_iota(jnp.int32, (tokens, tokens), 0) < (
        lax.broadcasted_iota(jnp.int32, (tokens, tokens), 1)
    )
    position = jnp.dot(
        named.astype(jnp.bfloat16),
        jnp.where(earlier, 1.0, 0.0).astype(jnp.bfloat16),
        preferred_element_type=jnp.float32,
    )
    placing = jnp.where(position == slot_place.astype(jnp.float32), named, 0.0)
    rest = weighted * placing
    for i in range(TERMS):
        term = rest.astype(jnp.bfloat16)
        table[i] = term
        rest = rest - term.astype(jnp.float32)
    table[TERMS] = placing.astype(jnp.bfloat16)

    def sent(ref, count, sem):
        if count:
            part = ref.at[pl.ds(0, count)]
            pltpu.make_async_copy(part, part, sem).wait()

    def z_wait(s):
        z_copy(s, t, 0).wait_recv()

    def z_pass(i):
        held = order[i][1]
        for s, to in relay[i]:
            if s != held:
                z_wait(s)
            held = s
            z_copy(s, to, 1).start()

    def z_drain(i):
        sent(tokens_in, len(own[i]), z_send.at[0])
        sent(tokens_in, len(relay[i]), z_send.at[1])

    def place(b, s, source):
        return (b * nt + s) * ne + source

    def f_copy(s, j, k):
        chip = lax.rem(e // PAIR + k // PAIR, nx)
        to = chip * PAIR + lax.rem(e + k, PAIR)
        return pltpu.make_async_remote_copy(
            src_ref=packed.at[s, to],
            dst_ref=feats.at[place(d, s, e)],
            send_sem=f_send.at[0],
            recv_sem=f_recv.at[d, s, e // PAIR],
            device_id=(lax.rem(d + j, nd), to, t),
            device_id_type=MESH,
        )

    def spread(s):
        packed[s] = (
            jnp.dot(table[TERMS], tokens_in[s], preferred_element_type=jnp.float32)
            .astype(jnp.bfloat16)
            .reshape(ne, CAP, width)
        )
        for k in range(1, ne):
            f_copy(s, 0, k).start()
        for j in range(1, nd):
            for k in range(PAIR):
                f_copy(s, j, k).start()
        feats[place(d, s, e)] = packed[s, e]

    def spread_far(s):
        for j in range(1, nd):
            for k in range(PAIR, ne):
                f_copy(s, j, k).start()

    def f_arrive(g, s):
        b, base = group(g)
        count = PAIR - 1 if isinstance(g, int) and g == 0 else PAIR
        block = feats.at[pl.ds(place(b, s, base), count)]
        pltpu.make_async_copy(block, block, f_recv.at[b, s, base // PAIR]).wait()

    def gate_up(gs, k, p=None):
        s = shard[k]
        columns = slice(None) if p is None else slice(p * share, (p + 1) * share)
        x = [
            feats[pl.ds(place(b, s, base), PAIR)].reshape(rows, width)
            for b, base in map(group, gs)
        ]
        x = jnp.concatenate(x) if len(gs) > 1 else x[0]
        here = slice(0, rows * len(gs))
        gate = jnp.dot(x, gate_up_w[s, 0, :, columns], preferred_element_type=jnp.float32)
        up = jnp.dot(x, gate_up_w[s, 1, :, columns], preferred_element_type=jnp.float32)
        if k == 0:
            gate_acc[here, columns] = gate
            up_acc[here, columns] = up
        else:
            gate_acc[here, columns] += gate
            up_acc[here, columns] += up

    def unit_place(b, s, base):
        return (b * nt + s) * nx + base // PAIR

    def activate(gs, p):
        for i, g in enumerate(gs):
            b, base = group(g)
            here, columns = pl.ds(i * rows, rows), pl.ds(p * share, share)
            gate = gate_acc[here, columns]
            value = gate / (1.0 + jnp.exp(-gate)) * up_acc[here, columns]
            acts[unit_place(b, t, base), p] = value.astype(jnp.bfloat16)
            u_own(g, p)

    def u_copy(g, s, to, sem, p=None):
        b, base = group(g)
        block = acts.at[unit_place(b, s, base)]
        if p is not None:
            block = block.at[p]
        return pltpu.make_async_remote_copy(
            src_ref=block,
            dst_ref=block,
            send_sem=u_send.at[sem],
            recv_sem=u_recv.at[g, s],
            device_id=(d, e, to),
            device_id_type=MESH,
        )

    def patient(i):
        return [to for to in own[i] if i in (0, nt - 1) and abs(to - i) == 1 and len(own[i]) > 1]

    def u_own(g, p):
        def act(i):
            for to in own[i]:
                if to not in patient(i):
                    u_copy(g, i, to, 0, p).start()

        per_place(act)

    def u_late(gs):
        def act(i):
            for g in gs:
                for to in patient(i):
                    u_copy(g, i, to, 0).start()

        per_place(act)

    def u_pass(gs, near):
        def act(i):
            for g in gs:
                held = None
                for s, to in relay[i]:
                    if (abs(s - i) == 1) == near:
                        copy = u_copy(g, s, to, 1)
                        if s != held:
                            copy.wait_recv()
                        held = s
                        copy.start()

        with jax.named_scope("pass_near" if near else "pass_far"):
            per_place(act)

    def u_take(g, s, skip):
        @pl.when(skip == 0)
        def _():
            u_copy(g, s, t, 0).wait_recv()

    def u_drain(i):
        sent(acts, groups * len(own[i]), u_send.at[0])
        sent(acts, groups * len(relay[i]), u_send.at[1])

    def down(gs, s, first, columns=slice(None)):
        h = [
            jnp.concatenate([acts[unit_place(b, s, base), p] for p in range(parts)], axis=1)
            for b, base in map(group, gs)
        ]
        h = jnp.concatenate(h) if len(gs) > 1 else h[0]
        value = jnp.dot(h, down_w[s, :, columns], preferred_element_type=jnp.float32)
        for i, g in enumerate(gs):
            part = value[i * rows : (i + 1) * rows]
            if first:
                down_acc[g, :, columns] = part
            else:
                down_acc[g, :, columns] += part

    def ret_copy(g, c, columns):
        b, base = group(g)
        return pltpu.make_async_remote_copy(
            src_ref=outgoing.at[b * ne + base + c, :, columns],
            dst_ref=returned.at[d * ne + e, :, columns],
            send_sem=ret_send.at[0],
            recv_sem=ret_recv.at[d, e // PAIR],
            device_id=(b, base + c, t),
            device_id_type=MESH,
        )

    def give_back(g, start=0, size=width):
        b, base = group(g)
        columns = pl.ds(start, size)
        first = pl.multiple_of(b * ne + base, PAIR)
        outgoing[pl.ds(first, PAIR), :, columns] = (
            down_acc[g, :, columns].astype(jnp.bfloat16).reshape(PAIR, CAP, size)
        )
        for c in range(PAIR):
            here = (b == d) & (base + c == e)

            @pl.when(jnp.logical_not(here))
            def _():
                ret_copy(g, c, columns).start()

            @pl.when(here)
            def _():
                returned[d * ne + e, :, columns] = outgoing[d * ne + e, :, columns]

    def ret_arrive(g, count):
        b, base = group(g)
        block = returned.at[pl.ds(b * ne + base, count)]
        pltpu.make_async_copy(block, block, ret_recv.at[b, base // PAIR]).wait()

    spread(t)
    spread_far(t)

    def first_batch(k):
        with jax.named_scope("f_arrive"):
            f_arrive(0, shard[k])
        with jax.named_scope("w_arrive"):
            pltpu.make_async_copy(
                gate_up_w.at[shard[k]], gate_up_w.at[shard[k]], w_sem.at[shard[k]]
            ).wait()
        for p in range(parts) if k == nt - 1 else (None,):
            with jax.named_scope("gate_up"):
                gate_up((0,), k, p)
            if p is not None:
                with jax.named_scope("activate"):
                    activate((0,), p)

    first_batch(0)
    busy = functools.reduce(jnp.logical_or, [t == i for i in range(nt) if relay[i]], t < 0)
    with jax.named_scope("z_arrive"):
        z_wait(shard[1])
        per_place(z_pass)
    with jax.named_scope("spread"):
        spread(shard[1])

    @pl.when(jnp.logical_not(busy))
    def _():
        first_batch(1)

    for k in range(2, nt):
        with jax.named_scope("z_arrive"):
            @pl.when(passed[k] == 0)
            def _():
                z_wait(shard[k])
        with jax.named_scope("spread"):
            spread(shard[k])

    @pl.when(busy)
    def _():
        first_batch(1)

    for k in range(2, nt):
        first_batch(k)
    for k in range(1, nt):
        spread_far(shard[k])

    def later_batch(index, gs):
        for p in range(parts):
            for k in range(nt):
                if p == 0:
                    with jax.named_scope("f_arrive"):
                        for g in gs:
                            f_arrive(g, shard[k])
                with jax.named_scope("gate_up"):
                    gate_up(gs, k, p)
                if p == 0 and k == nt - 2:
                    @pl.when(index == 2)
                    def _():
                        u_pass((0,), False)

                    @pl.when(index > 2)
                    def _():
                        of_batch(index - 2, lambda old: u_pass(old, True))
            with jax.named_scope("activate"):
                activate(gs, p)
        of_batch(index - 1, u_late)

        @pl.when(index == 1)
        def _():
            u_pass((0,), True)

        if not listed:
            @pl.when(index > 1)
            def _():
                of_batch(index - 1, lambda old: u_pass(old, False))

    def pair_batch(index, carry):
        later_batch(index, (2 * index - 1, 2 * index))
        return carry

    lax.fori_loop(1, (groups + 1) // 2, pair_batch, 0)
    if groups % 2 == 0:
        later_batch(batches - 1, (groups - 1,))
    of_batch(batches - 1, u_late)

    pltpu.make_async_copy(down_w, down_w, w_sem.at[nt]).wait()

    def finish(q, carry):
        if batches > 1:
            @pl.when(q == 2)
            def _():
                of_batch(batches - 2, lambda gs: u_pass(gs, batches > 2))

        @pl.when(q == min(3, batches))
        def _():
            of_batch(batches - 1, lambda gs: u_pass(gs, True))

        @pl.when(q == min(3, batches))
        def _():
            of_batch(batches - 1, lambda gs: u_pass(gs, False))

        def step(k, gs):
            if k:
                with jax.named_scope("u_arrive%d" % k):
                    for g in gs:
                        u_take(g, shard[k], passed[k])
            with jax.named_scope("down"):
                down(gs, shard[k], k == 0)
            if k == nt - 1:
                for g in gs:
                    give_back(g)

        for k in range(nt):
            @pl.when((q >= k) & (q - k < batches))
            def _():
                of_batch(q - k, functools.partial(step, k))

        return carry

    def listed_step(index, end_k, mid_k, last):
        gs = ((0,), (1, 2), (3,))[index]
        s = jnp.where(at_end, shard[end_k], shard[mid_k])
        if end_k:
            with jax.named_scope("u_arrive%d%d%d" % (index, end_k, mid_k)):
                for g in gs:
                    u_take(g, s, jnp.where(at_end, 0, passed[mid_k]))
        with jax.named_scope("down"):
            cuts = 2 if last and index and width % 256 == 0 else 1
            for c in range(cuts):
                size = width // cuts
                down(gs, s, end_k == 0, slice(c * size, (c + 1) * size))
                if last:
                    for g in gs:
                        give_back(g, c * size, size)

    if listed:
        for index in range(3):
            listed_step(index, 0, 0, False)
        middle, final = (1, 2), (3,)
        u_pass(middle, False)
        listed_step(0, 1, 1, False)
        listed_step(1, 1, 3, False)

        @pl.when(jnp.logical_not(far_corner))
        def _():
            u_pass(middle, True)

        listed_step(0, 3, 3, False)
        listed_step(0, 2, 2, True)

        @pl.when(jnp.logical_not(far_corner))
        def _():
            listed_step(1, 3, 1, False)
            u_pass(final, True)
            listed_step(2, 1, 1, False)
            u_pass(final, False)
            listed_step(1, 2, 2, True)
            listed_step(2, 2, 3, False)
            listed_step(2, 3, 2, True)

        @pl.when(far_corner)
        def _():
            u_pass(final, True)
            listed_step(2, 1, 1, False)
            u_pass(final, False)
            listed_step(2, 2, 3, False)
            u_pass(middle, True)
            listed_step(2, 3, 2, True)
            listed_step(1, 3, 1, False)
            listed_step(1, 2, 2, True)
    else:
        lax.fori_loop(0, batches + nt - 1, finish, 0)

    total[...] = jnp.zeros((tokens, width), jnp.float32)

    def combine(g):
        with jax.named_scope("ret_arrive"):
            ret_arrive(g, PAIR - 1 if isinstance(g, int) else PAIR)
        with jax.named_scope("combine"):
            b, base = group(g)
            back = returned[pl.ds(b * ne + base, PAIR)].reshape(rows, width)
            places = pl.ds(pl.multiple_of(base * CAP, rows), rows)
            for i in range(TERMS):
                total[...] += lax.dot_general(
                    table[i, places], back, (((0,), (0,)), ((), ())),
                    preferred_element_type=jnp.float32,
                )

    combine(0)
    lax.fori_loop(1, groups, lambda g, carry: (combine(g), carry)[1], 0)
    out_ref[...] = total[...].astype(jnp.bfloat16)

    with jax.named_scope("drain"):
        per_place(z_drain)
        sent(feats, nt * (nd * ne - 1), f_send.at[0])
        per_place(u_drain)
        sent(outgoing, nd * ne - 1, ret_send.at[0])


def body(mesh, hidden_states, chosen_experts, choice_weights, gate_proj, up_proj, down_proj):
    nd, ne, nt = mesh.shape["dp"], mesh.shape["expert"], mesh.shape["tensor"]
    tokens, width = hidden_states.shape
    units = gate_proj.shape[2]
    slots = ne * CAP
    rows = PAIR * CAP
    groups = nd * ne // PAIR
    parts = 1 if units % 256 else 2
    vmem = pl.BlockSpec(memory_space=pltpu.VMEM)
    hbm = pl.BlockSpec(memory_space=pltpu.HBM)
    bf16, f32, dma = jnp.bfloat16, jnp.float32, pltpu.SemaphoreType.DMA
    operands = [
        pltpu.with_memory_space_constraint(x, pltpu.HBM)
        for x in (hidden_states, chosen_experts.T, choice_weights.T, gate_proj, up_proj, down_proj)
    ]
    return pl.pallas_call(
        functools.partial(kernel, nd, ne, nt),
        out_shape=jax.ShapeDtypeStruct((tokens, width), bf16),
        in_specs=[hbm] * 6,
        out_specs=vmem,
        scratch_shapes=[
            pltpu.VMEM((nt, tokens, width), bf16),
            pltpu.VMEM(chosen_experts.shape[::-1], jnp.int32),
            pltpu.VMEM(choice_weights.shape[::-1], f32),
            pltpu.VMEM((nt, ne, CAP, width), bf16),
            pltpu.VMEM((nd * nt * ne, CAP, width), bf16),
            pltpu.VMEM((groups * nt, parts, rows, units // parts), bf16),
            pltpu.VMEM((nt, 2, width, units), bf16),
            pltpu.VMEM((nt, units, width), bf16),
            pltpu.VMEM((2 * rows, units), f32),
            pltpu.VMEM((2 * rows, units), f32),
            pltpu.VMEM((groups, rows, width), f32),
            pltpu.VMEM((nd * ne, CAP, width), bf16),
            pltpu.VMEM((nd * ne, CAP, width), bf16),
            pltpu.VMEM((TERMS + 1, slots, tokens), bf16),
            pltpu.VMEM((tokens, width), f32),
            dma((3,)),
            dma((nt + 1,)),
            dma((2,)),
            dma((nt,)),
            dma((1,)),
            dma((nd, nt, ne // PAIR)),
            dma((2,)),
            dma((groups, nt)),
            dma((1,)),
            dma((nd, ne // PAIR)),
        ],
        compiler_params=pltpu.CompilerParams(
            collective_id=0, has_side_effects=True, vmem_limit_bytes=48 << 20
        ),
        name="experts",
    )(*operands)


def solution(mesh):
    in_specs = (
        P(("dp", "expert"), "tensor"),
        P(("dp", "expert"), None),
        P(("dp", "expert"), None),
        P("expert", None, ("dp", "tensor")),
        P("expert", None, ("dp", "tensor")),
        P("expert", "dp", "tensor"),
    )
    out_specs = P(("dp", "expert"), "tensor")
    return jax.shard_map(
        functools.partial(body, mesh), mesh=mesh, in_specs=in_specs, out_specs=out_specs,
        check_vma=False,
    )
```

```python
import functools

import jax
import jax.numpy as jnp
from jax import lax
from jax.experimental import pallas as pl
from jax.experimental.pallas import tpu as pltpu
from jax.sharding import PartitionSpec as P

CAP = 16
PAIR = 2
HOP = 2
TERMS = 2
MESH = pl.DeviceIdType.MESH


def routes(nt):
    own, relay = [[] for _ in range(nt)], [[] for _ in range(nt)]
    for side in (-1, 1):
        end = nt - 1 if side > 0 else 0
        for s in range(nt):
            for dist in range(1, abs(end - s) + 1):
                to = s + side * dist
                back = 1 if to == end else dist - (dist - 1) // HOP * HOP
                holder = to - side * back
                if holder == s:
                    own[s].append(to)
                else:
                    relay[holder].append((s, to))
    for r in range(nt):
        own[r].sort(key=lambda to: -abs(to - r))
        relay[r].sort(key=lambda pair: abs(pair[0] - r))
    return own, relay


def kernel(
    nd, ne, nt,
    hidden_hbm, ids_hbm, weights_hbm, gate_hbm, up_hbm, down_hbm, out_ref,
    tokens_in, ids_ref, weights_ref, packed, feats, acts, gate_up_w, down_w,
    gate_acc, up_acc, down_acc, outgoing, returned, table, total,
    in_sem, w_sem, z_send, z_recv, f_send, f_recv, u_send, u_recv,
    ret_send, ret_recv,
):
    d, e, t = lax.axis_index("dp"), lax.axis_index("expert"), lax.axis_index("tensor")
    tokens, width = tokens_in.shape[1:]
    slots = ne * CAP
    units = gate_up_w.shape[3]
    parts = acts.shape[1]
    share = units // parts
    nx = ne // PAIR
    groups = nd * nx
    rows = PAIR * CAP
    own, relay = routes(nt)

    def pick(values):
        value = values[0]
        for i in range(1, nt):
            value = jnp.where(t == i, values[i], value)
        return value

    order = [
        sorted(range(nt), key=lambda s: (abs(s - i), abs(2 * s - nt + 1))) for i in range(nt)
    ]
    shard = [pick([order[i][k] for i in range(nt)]) for k in range(nt)]
    passed = [
        pick([int(any(s == order[i][k] for s, _ in relay[i])) for i in range(nt)])
        for k in range(nt)
    ]
    batches = 1 + groups // 2
    listed = nt == 4 and groups == 4
    far_corner = (d == nd - 1) & (e // PAIR == nx - 1)
    at_end = (t == 0) | (t == nt - 1)

    def of_batch(index, act):
        if isinstance(index, int):
            return act(tuple(range(max(2 * index - 1, 0), min(2 * index + 1, groups))))

        @pl.when(index == 0)
        def _():
            act((0,))

        if batches > 2 - groups % 2:
            @pl.when((index > 0) & (2 * index < groups))
            def _():
                act((2 * index - 1, 2 * index))

        if groups % 2 == 0:
            @pl.when(index == batches - 1)
            def _():
                act((groups - 1,))

    def group(g):
        j, k = g // nx, lax.rem(g, nx)
        b = lax.rem(d + j, nd)
        base = pl.multiple_of(lax.rem(e // PAIR + k, nx) * PAIR, PAIR)
        return b, base

    barrier = pltpu.get_barrier_semaphore()
    for j in range(nd):
        for k in range(ne):
            if j or k:
                pl.semaphore_signal(
                    barrier, inc=1, device_id_type=MESH,
                    device_id=(lax.rem(d + j, nd), lax.rem(e + k, ne), t),
                )
    greeted = nd * ne - 1
    for k in range(-HOP, HOP + 1):
        if k:
            near = (t + k >= 0) & (t + k < nt)
            greeted += near.astype(jnp.int32)

            @pl.when(near)
            def _():
                pl.semaphore_signal(
                    barrier, inc=1, device_id=(d, e, t + k), device_id_type=MESH
                )
    inputs = (
        pltpu.make_async_copy(hidden_hbm, tokens_in.at[t], in_sem.at[2]),
        pltpu.make_async_copy(ids_hbm, ids_ref, in_sem.at[0]),
        pltpu.make_async_copy(weights_hbm, weights_ref, in_sem.at[1]),
    )
    for copy in inputs:
        copy.start()

    def gate_up_copy(i, s):
        return pltpu.make_async_copy(
            (gate_hbm, up_hbm)[i].at[0, pl.ds(pl.multiple_of(s * width, width), width)],
            gate_up_w.at[s, i],
            w_sem.at[s],
        )

    def down_copy(s):
        return pltpu.make_async_copy(
            down_hbm.at[0, pl.ds(pl.multiple_of(s * units, units), units)],
            down_w.at[s],
            w_sem.at[nt],
        )

    gate_up_copy(0, t).start()
    gate_up_copy(1, t).start()

    def per_place(act):
        for i in range(nt):
            @pl.when(t == i)
            def _():
                act(i)

    def z_copy(s, to, sem, source=None):
        return pltpu.make_async_remote_copy(
            src_ref=tokens_in.at[s] if source is None else source,
            dst_ref=tokens_in.at[s],
            send_sem=z_send.at[sem],
            recv_sem=z_recv.at[s],
            device_id=(d, e, to),
            device_id_type=MESH,
        )

    def z_own(i):
        for to in own[i]:
            z_copy(i, to, 0, hidden_hbm).start()

    with jax.named_scope("barrier"):
        pl.semaphore_wait(barrier, greeted)
    per_place(z_own)
    for copy in inputs:
        copy.wait()
    for k in range(1, nt):
        gate_up_copy(0, shard[k]).start()
        gate_up_copy(1, shard[k]).start()
    for k in range(nt):
        down_copy(shard[k]).start()

    slot = lax.broadcasted_iota(jnp.int32, (slots, tokens), 0)
    slot_expert = lax.shift_right_logical(slot, CAP.bit_length() - 1)
    slot_place = slot - slot_expert * CAP
    named = jnp.zeros((slots, tokens), jnp.float32)
    weighted = jnp.zeros((slots, tokens), jnp.float32)
    for row in range(ids_ref.shape[0]):
        match = ids_ref[row : row + 1, :] == slot_expert
        named = jnp.where(match, 1.0, named)
        weighted = jnp.where(match, weights_ref[row : row + 1, :], weighted)
    earlier = lax.broadcasted_iota(jnp.int32, (tokens, tokens), 0) < (
        lax.broadcasted_iota(jnp.int32, (tokens, tokens), 1)
    )
    position = jnp.dot(
        named.astype(jnp.bfloat16),
        jnp.where(earlier, 1.0, 0.0).astype(jnp.bfloat16),
        preferred_element_type=jnp.float32,
    )
    placing = jnp.where(position == slot_place.astype(jnp.float32), named, 0.0)
    rest = weighted * placing
    for i in range(TERMS):
        term = rest.astype(jnp.bfloat16)
        table[i] = term
        rest = rest - term.astype(jnp.float32)
    table[TERMS] = placing.astype(jnp.bfloat16)

    def sent(ref, count, sem):
        if count:
            part = ref.at[pl.ds(0, count)]
            pltpu.make_async_copy(part, part, sem).wait()

    def z_wait(s):
        z_copy(s, t, 0).wait_recv()

    def z_pass(i):
        held = order[i][1]
        for s, to in relay[i]:
            if s != held:
                z_wait(s)
            held = s
            z_copy(s, to, 1).start()

    def z_drain(i):
        sent(tokens_in, len(own[i]), z_send.at[0])
        sent(tokens_in, len(relay[i]), z_send.at[1])

    def place(b, s, source):
        return (b * nt + s) * ne + source

    def f_copy(s, j, k):
        chip = lax.rem(e // PAIR + k // PAIR, nx)
        to = chip * PAIR + lax.rem(e + k, PAIR)
        return pltpu.make_async_remote_copy(
            src_ref=packed.at[s, to],
            dst_ref=feats.at[place(d, s, e)],
            send_sem=f_send.at[0],
            recv_sem=f_recv.at[d, s, e // PAIR],
            device_id=(lax.rem(d + j, nd), to, t),
            device_id_type=MESH,
        )

    def spread(s):
        packed[s] = (
            jnp.dot(table[TERMS], tokens_in[s], preferred_element_type=jnp.float32)
            .astype(jnp.bfloat16)
            .reshape(ne, CAP, width)
        )
        for k in range(1, ne):
            f_copy(s, 0, k).start()
        for j in range(1, nd):
            for k in range(PAIR):
                f_copy(s, j, k).start()
        feats[place(d, s, e)] = packed[s, e]

    def spread_far(s):
        for j in range(1, nd):
            for k in range(PAIR, ne):
                f_copy(s, j, k).start()

    def f_arrive(g, s):
        b, base = group(g)
        count = PAIR - 1 if isinstance(g, int) and g == 0 else PAIR
        block = feats.at[pl.ds(place(b, s, base), count)]
        pltpu.make_async_copy(block, block, f_recv.at[b, s, base // PAIR]).wait()

    def gate_up(gs, k, p=None):
        s = shard[k]
        columns = slice(None) if p is None else slice(p * share, (p + 1) * share)
        x = [
            feats[pl.ds(place(b, s, base), PAIR)].reshape(rows, width)
            for b, base in map(group, gs)
        ]
        x = jnp.concatenate(x) if len(gs) > 1 else x[0]
        here = slice(0, rows * len(gs))
        gate = jnp.dot(x, gate_up_w[s, 0, :, columns], preferred_element_type=jnp.float32)
        up = jnp.dot(x, gate_up_w[s, 1, :, columns], preferred_element_type=jnp.float32)
        if k == 0:
            gate_acc[here, columns] = gate
            up_acc[here, columns] = up
        else:
            gate_acc[here, columns] += gate
            up_acc[here, columns] += up

    def unit_place(b, s, base):
        return (b * nt + s) * nx + base // PAIR

    def activate(gs, p):
        for i, g in enumerate(gs):
            b, base = group(g)
            here, columns = pl.ds(i * rows, rows), pl.ds(p * share, share)
            gate = gate_acc[here, columns]
            value = gate / (1.0 + jnp.exp(-gate)) * up_acc[here, columns]
            acts[unit_place(b, t, base), p] = value.astype(jnp.bfloat16)
            u_own(g, p)

    def u_copy(g, s, to, sem, p=None):
        b, base = group(g)
        block = acts.at[unit_place(b, s, base)]
        if p is not None:
            block = block.at[p]
        return pltpu.make_async_remote_copy(
            src_ref=block,
            dst_ref=block,
            send_sem=u_send.at[sem],
            recv_sem=u_recv.at[g, s],
            device_id=(d, e, to),
            device_id_type=MESH,
        )

    def patient(i):
        return [to for to in own[i] if i in (0, nt - 1) and abs(to - i) == 1 and len(own[i]) > 1]

    def u_own(g, p):
        def act(i):
            for to in own[i]:
                if to not in patient(i):
                    u_copy(g, i, to, 0, p).start()

        per_place(act)

    def u_late(gs):
        def act(i):
            for g in gs:
                for to in patient(i):
                    u_copy(g, i, to, 0).start()

        per_place(act)

    def u_pass(gs, near):
        def act(i):
            for g in gs:
                held = None
                for s, to in relay[i]:
                    if (abs(s - i) == 1) == near:
                        copy = u_copy(g, s, to, 1)
                        if s != held:
                            copy.wait_recv()
                        held = s
                        copy.start()

        with jax.named_scope("pass_near" if near else "pass_far"):
            per_place(act)

    def u_take(g, s, skip):
        @pl.when(skip == 0)
        def _():
            u_copy(g, s, t, 0).wait_recv()

    def u_drain(i):
        sent(acts, groups * len(own[i]), u_send.at[0])
        sent(acts, groups * len(relay[i]), u_send.at[1])

    def down(gs, s, first, columns=slice(None)):
        h = [
            jnp.concatenate([acts[unit_place(b, s, base), p] for p in range(parts)], axis=1)
            for b, base in map(group, gs)
        ]
        h = jnp.concatenate(h) if len(gs) > 1 else h[0]
        value = jnp.dot(h, down_w[s, :, columns], preferred_element_type=jnp.float32)
        for i, g in enumerate(gs):
            part = value[i * rows : (i + 1) * rows]
            if first:
                down_acc[g, :, columns] = part
            else:
                down_acc[g, :, columns] += part

    def ret_copy(g, c, columns):
        b, base = group(g)
        return pltpu.make_async_remote_copy(
            src_ref=outgoing.at[b * ne + base + c, :, columns],
            dst_ref=returned.at[d * ne + e, :, columns],
            send_sem=ret_send.at[0],
            recv_sem=ret_recv.at[d, e // PAIR],
            device_id=(b, base + c, t),
            device_id_type=MESH,
        )

    def give_back(g, start=0, size=width):
        b, base = group(g)
        columns = pl.ds(start, size)
        first = pl.multiple_of(b * ne + base, PAIR)
        outgoing[pl.ds(first, PAIR), :, columns] = (
            down_acc[g, :, columns].astype(jnp.bfloat16).reshape(PAIR, CAP, size)
        )
        for c in range(PAIR):
            here = (b == d) & (base + c == e)

            @pl.when(jnp.logical_not(here))
            def _():
                ret_copy(g, c, columns).start()

            @pl.when(here)
            def _():
                returned[d * ne + e, :, columns] = outgoing[d * ne + e, :, columns]

    def ret_arrive(g, count):
        b, base = group(g)
        block = returned.at[pl.ds(b * ne + base, count)]
        pltpu.make_async_copy(block, block, ret_recv.at[b, base // PAIR]).wait()

    spread(t)
    spread_far(t)

    def first_batch(k):
        with jax.named_scope("f_arrive"):
            f_arrive(0, shard[k])
        with jax.named_scope("w_arrive"):
            pltpu.make_async_copy(
                gate_up_w.at[shard[k]], gate_up_w.at[shard[k]], w_sem.at[shard[k]]
            ).wait()
        for p in range(parts) if k == nt - 1 else (None,):
            with jax.named_scope("gate_up"):
                gate_up((0,), k, p)
            if p is not None:
                with jax.named_scope("activate"):
                    activate((0,), p)

    first_batch(0)
    busy = functools.reduce(jnp.logical_or, [t == i for i in range(nt) if relay[i]], t < 0)
    with jax.named_scope("z_arrive"):
        z_wait(shard[1])
        per_place(z_pass)
    with jax.named_scope("spread"):
        spread(shard[1])

    @pl.when(jnp.logical_not(busy))
    def _():
        first_batch(1)

    for k in range(2, nt):
        with jax.named_scope("z_arrive"):
            @pl.when(passed[k] == 0)
            def _():
                z_wait(shard[k])
        with jax.named_scope("spread"):
            spread(shard[k])

    @pl.when(busy)
    def _():
        first_batch(1)

    for k in range(2, nt):
        first_batch(k)
    for k in range(1, nt):
        spread_far(shard[k])

    def later_batch(index, gs):
        for p in range(parts):
            for k in range(nt):
                if p == 0:
                    with jax.named_scope("f_arrive"):
                        for g in gs:
                            f_arrive(g, shard[k])
                with jax.named_scope("gate_up"):
                    gate_up(gs, k, p)
                if p == 0 and k == nt - 2:
                    @pl.when(index == 2)
                    def _():
                        u_pass((0,), False)

                    @pl.when(index > 2)
                    def _():
                        of_batch(index - 2, lambda old: u_pass(old, True))
            with jax.named_scope("activate"):
                activate(gs, p)
        of_batch(index - 1, u_late)

        @pl.when(index == 1)
        def _():
            u_pass((0,), True)

        if not listed:
            @pl.when(index > 1)
            def _():
                of_batch(index - 1, lambda old: u_pass(old, False))

    def pair_batch(index, carry):
        later_batch(index, (2 * index - 1, 2 * index))
        return carry

    lax.fori_loop(1, (groups + 1) // 2, pair_batch, 0)
    if groups % 2 == 0:
        later_batch(batches - 1, (groups - 1,))
    of_batch(batches - 1, u_late)

    pltpu.make_async_copy(down_w, down_w, w_sem.at[nt]).wait()

    def finish(q, carry):
        if batches > 1:
            @pl.when(q == 2)
            def _():
                of_batch(batches - 2, lambda gs: u_pass(gs, batches > 2))

        @pl.when(q == min(3, batches))
        def _():
            of_batch(batches - 1, lambda gs: u_pass(gs, True))

        @pl.when(q == min(3, batches))
        def _():
            of_batch(batches - 1, lambda gs: u_pass(gs, False))

        def step(k, gs):
            if k:
                with jax.named_scope("u_arrive%d" % k):
                    for g in gs:
                        u_take(g, shard[k], passed[k])
            with jax.named_scope("down"):
                down(gs, shard[k], k == 0)
            if k == nt - 1:
                for g in gs:
                    give_back(g)

        for k in range(nt):
            @pl.when((q >= k) & (q - k < batches))
            def _():
                of_batch(q - k, functools.partial(step, k))

        return carry

    def listed_step(index, end_k, mid_k, last):
        gs = ((0,), (1, 2), (3,))[index]
        s = jnp.where(at_end, shard[end_k], shard[mid_k])
        if end_k:
            with jax.named_scope("u_arrive%d%d%d" % (index, end_k, mid_k)):
                for g in gs:
                    u_take(g, s, jnp.where(at_end, 0, passed[mid_k]))
        with jax.named_scope("down"):
            cuts = 2 if last and index and width % 256 == 0 else 1
            for c in range(cuts):
                size = width // cuts
                down(gs, s, end_k == 0, slice(c * size, (c + 1) * size))
                if last:
                    for g in gs:
                        give_back(g, c * size, size)

    if listed:
        for index in range(3):
            listed_step(index, 0, 0, False)
        middle, final = (1, 2), (3,)
        u_pass(middle, False)
        listed_step(0, 1, 1, False)
        listed_step(1, 1, 3, False)

        @pl.when(jnp.logical_not(far_corner))
        def _():
            u_pass(middle, True)

        listed_step(0, 3, 3, False)
        listed_step(0, 2, 2, True)

        @pl.when(jnp.logical_not(far_corner))
        def _():
            listed_step(1, 3, 1, False)
            u_pass(final, True)
            listed_step(2, 1, 1, False)
            u_pass(final, False)
            listed_step(1, 2, 2, True)
            listed_step(2, 2, 3, False)
            listed_step(2, 3, 2, True)

        @pl.when(far_corner)
        def _():
            u_pass(final, True)
            listed_step(2, 1, 1, False)
            u_pass(final, False)
            listed_step(2, 2, 3, False)
            u_pass(middle, True)
            listed_step(2, 3, 2, True)
            listed_step(1, 3, 1, False)
            listed_step(1, 2, 2, True)
    else:
        lax.fori_loop(0, batches + nt - 1, finish, 0)

    total[...] = jnp.zeros((tokens, width), jnp.float32)

    def combine(g):
        with jax.named_scope("ret_arrive"):
            ret_arrive(g, PAIR - 1 if isinstance(g, int) else PAIR)
        with jax.named_scope("combine"):
            b, base = group(g)
            back = returned[pl.ds(b * ne + base, PAIR)].reshape(rows, width)
            places = pl.ds(pl.multiple_of(base * CAP, rows), rows)
            for i in range(TERMS):
                total[...] += lax.dot_general(
                    table[i, places], back, (((0,), (0,)), ((), ())),
                    preferred_element_type=jnp.float32,
                )

    combine(0)
    corner = lax.rem(nd - 1 - d, nd) * nx + lax.rem(nx - 1 - e // PAIR, nx)
    corner = jnp.where(corner == 0, groups - 1, corner)

    def combine_next(i, carry):
        combine(1 + lax.rem(corner - 1 + i, groups - 1))
        return carry

    lax.fori_loop(1, groups, combine_next, 0)
    out_ref[...] = total[...].astype(jnp.bfloat16)

    with jax.named_scope("drain"):
        per_place(z_drain)
        sent(feats, nt * (nd * ne - 1), f_send.at[0])
        per_place(u_drain)
        sent(outgoing, nd * ne - 1, ret_send.at[0])


def body(mesh, hidden_states, chosen_experts, choice_weights, gate_proj, up_proj, down_proj):
    nd, ne, nt = mesh.shape["dp"], mesh.shape["expert"], mesh.shape["tensor"]
    tokens, width = hidden_states.shape
    units = gate_proj.shape[2]
    slots = ne * CAP
    rows = PAIR * CAP
    groups = nd * ne // PAIR
    parts = 1 if units % 256 else 2
    vmem = pl.BlockSpec(memory_space=pltpu.VMEM)
    hbm = pl.BlockSpec(memory_space=pltpu.HBM)
    bf16, f32, dma = jnp.bfloat16, jnp.float32, pltpu.SemaphoreType.DMA
    operands = [
        pltpu.with_memory_space_constraint(x, pltpu.HBM)
        for x in (hidden_states, chosen_experts.T, choice_weights.T, gate_proj, up_proj, down_proj)
    ]
    return pl.pallas_call(
        functools.partial(kernel, nd, ne, nt),
        out_shape=jax.ShapeDtypeStruct((tokens, width), bf16),
        in_specs=[hbm] * 6,
        out_specs=vmem,
        scratch_shapes=[
            pltpu.VMEM((nt, tokens, width), bf16),
            pltpu.VMEM(chosen_experts.shape[::-1], jnp.int32),
            pltpu.VMEM(choice_weights.shape[::-1], f32),
            pltpu.VMEM((nt, ne, CAP, width), bf16),
            pltpu.VMEM((nd * nt * ne, CAP, width), bf16),
            pltpu.VMEM((groups * nt, parts, rows, units // parts), bf16),
            pltpu.VMEM((nt, 2, width, units), bf16),
            pltpu.VMEM((nt, units, width), bf16),
            pltpu.VMEM((2 * rows, units), f32),
            pltpu.VMEM((2 * rows, units), f32),
            pltpu.VMEM((groups, rows, width), f32),
            pltpu.VMEM((nd * ne, CAP, width), bf16),
            pltpu.VMEM((nd * ne, CAP, width), bf16),
            pltpu.VMEM((TERMS + 1, slots, tokens), bf16),
            pltpu.VMEM((tokens, width), f32),
            dma((3,)),
            dma((nt + 1,)),
            dma((2,)),
            dma((nt,)),
            dma((1,)),
            dma((nd, nt, ne // PAIR)),
            dma((2,)),
            dma((groups, nt)),
            dma((1,)),
            dma((nd, ne // PAIR)),
        ],
        compiler_params=pltpu.CompilerParams(
            collective_id=0, has_side_effects=True, vmem_limit_bytes=48 << 20
        ),
        name="experts",
    )(*operands)


def solution(mesh):
    in_specs = (
        P(("dp", "expert"), "tensor"),
        P(("dp", "expert"), None),
        P(("dp", "expert"), None),
        P("expert", None, ("dp", "tensor")),
        P("expert", None, ("dp", "tensor")),
        P("expert", "dp", "tensor"),
    )
    out_specs = P(("dp", "expert"), "tensor")
    return jax.shard_map(
        functools.partial(body, mesh), mesh=mesh, in_specs=in_specs, out_specs=out_specs,
        check_vma=False,
    )
```

```python
import functools

import jax
import jax.numpy as jnp
from jax import lax
from jax.experimental import pallas as pl
from jax.experimental.pallas import tpu as pltpu
from jax.sharding import PartitionSpec as P

CAP = 16
PAIR = 2
HOP = 2
TERMS = 2
MESH = pl.DeviceIdType.MESH


def routes(nt):
    own, relay = [[] for _ in range(nt)], [[] for _ in range(nt)]
    for side in (-1, 1):
        end = nt - 1 if side > 0 else 0
        for s in range(nt):
            for dist in range(1, abs(end - s) + 1):
                to = s + side * dist
                back = 1 if to == end else dist - (dist - 1) // HOP * HOP
                holder = to - side * back
                if holder == s:
                    own[s].append(to)
                else:
                    relay[holder].append((s, to))
    for r in range(nt):
        own[r].sort(key=lambda to: -abs(to - r))
        relay[r].sort(key=lambda pair: abs(pair[0] - r))
    return own, relay


def kernel(
    nd, ne, nt,
    hidden_hbm, ids_hbm, weights_hbm, gate_hbm, up_hbm, down_hbm, out_ref,
    tokens_in, ids_ref, weights_ref, packed, feats, acts, gate_up_w, down_w,
    gate_acc, up_acc, down_acc, outgoing, returned, table, total,
    in_sem, w_sem, z_send, z_recv, f_send, f_recv, u_send, u_recv,
    ret_send, ret_recv,
):
    d, e, t = lax.axis_index("dp"), lax.axis_index("expert"), lax.axis_index("tensor")
    tokens, width = tokens_in.shape[1:]
    slots = ne * CAP
    units = gate_up_w.shape[3]
    parts = acts.shape[1]
    share = units // parts
    nx = ne // PAIR
    groups = nd * nx
    rows = PAIR * CAP
    own, relay = routes(nt)

    def pick(values):
        value = values[0]
        for i in range(1, nt):
            value = jnp.where(t == i, values[i], value)
        return value

    order = [
        sorted(range(nt), key=lambda s: (abs(s - i), abs(2 * s - nt + 1))) for i in range(nt)
    ]
    shard = [pick([order[i][k] for i in range(nt)]) for k in range(nt)]
    passed = [
        pick([int(any(s == order[i][k] for s, _ in relay[i])) for i in range(nt)])
        for k in range(nt)
    ]
    batches = 1 + groups // 2
    listed = nt == 4 and groups == 4
    far_corner = (d == nd - 1) & (e // PAIR == nx - 1)
    at_end = (t == 0) | (t == nt - 1)

    def of_batch(index, act):
        if isinstance(index, int):
            return act(tuple(range(max(2 * index - 1, 0), min(2 * index + 1, groups))))

        @pl.when(index == 0)
        def _():
            act((0,))

        if batches > 2 - groups % 2:
            @pl.when((index > 0) & (2 * index < groups))
            def _():
                act((2 * index - 1, 2 * index))

        if groups % 2 == 0:
            @pl.when(index == batches - 1)
            def _():
                act((groups - 1,))

    def group(g):
        j, k = g // nx, lax.rem(g, nx)
        b = lax.rem(d + j, nd)
        base = pl.multiple_of(lax.rem(e // PAIR + k, nx) * PAIR, PAIR)
        return b, base

    barrier = pltpu.get_barrier_semaphore()
    for j in range(nd):
        for k in range(ne):
            if j or k:
                pl.semaphore_signal(
                    barrier, inc=1, device_id_type=MESH,
                    device_id=(lax.rem(d + j, nd), lax.rem(e + k, ne), t),
                )
    greeted = nd * ne - 1
    for k in range(-HOP, HOP + 1):
        if k:
            near = (t + k >= 0) & (t + k < nt)
            greeted += near.astype(jnp.int32)

            @pl.when(near)
            def _():
                pl.semaphore_signal(
                    barrier, inc=1, device_id=(d, e, t + k), device_id_type=MESH
                )
    inputs = (
        pltpu.make_async_copy(hidden_hbm, tokens_in.at[t], in_sem.at[2]),
        pltpu.make_async_copy(ids_hbm, ids_ref, in_sem.at[0]),
        pltpu.make_async_copy(weights_hbm, weights_ref, in_sem.at[1]),
    )
    for copy in inputs:
        copy.start()

    def gate_up_copy(i, s):
        return pltpu.make_async_copy(
            (gate_hbm, up_hbm)[i].at[0, pl.ds(pl.multiple_of(s * width, width), width)],
            gate_up_w.at[s, i],
            w_sem.at[s],
        )

    def down_copy(s):
        return pltpu.make_async_copy(
            down_hbm.at[0, pl.ds(pl.multiple_of(s * units, units), units)],
            down_w.at[s],
            w_sem.at[nt],
        )

    gate_up_copy(0, t).start()
    gate_up_copy(1, t).start()

    def per_place(act):
        for i in range(nt):
            @pl.when(t == i)
            def _():
                act(i)

    def z_copy(s, to, sem, source=None):
        return pltpu.make_async_remote_copy(
            src_ref=tokens_in.at[s] if source is None else source,
            dst_ref=tokens_in.at[s],
            send_sem=z_send.at[sem],
            recv_sem=z_recv.at[s],
            device_id=(d, e, to),
            device_id_type=MESH,
        )

    def z_own(i):
        for to in own[i]:
            z_copy(i, to, 0, hidden_hbm).start()

    with jax.named_scope("barrier"):
        pl.semaphore_wait(barrier, greeted)
    per_place(z_own)
    for copy in inputs:
        copy.wait()
    for k in range(1, nt):
        gate_up_copy(0, shard[k]).start()
        gate_up_copy(1, shard[k]).start()
    for k in range(nt):
        down_copy(shard[k]).start()

    slot = lax.broadcasted_iota(jnp.int32, (slots, tokens), 0)
    slot_expert = lax.shift_right_logical(slot, CAP.bit_length() - 1)
    slot_place = slot - slot_expert * CAP
    named = jnp.zeros((slots, tokens), jnp.float32)
    weighted = jnp.zeros((slots, tokens), jnp.float32)
    for row in range(ids_ref.shape[0]):
        match = ids_ref[row : row + 1, :] == slot_expert
        named = jnp.where(match, 1.0, named)
        weighted = jnp.where(match, weights_ref[row : row + 1, :], weighted)
    earlier = lax.broadcasted_iota(jnp.int32, (tokens, tokens), 0) < (
        lax.broadcasted_iota(jnp.int32, (tokens, tokens), 1)
    )
    position = jnp.dot(
        named.astype(jnp.bfloat16),
        jnp.where(earlier, 1.0, 0.0).astype(jnp.bfloat16),
        preferred_element_type=jnp.float32,
    )
    placing = jnp.where(position == slot_place.astype(jnp.float32), named, 0.0)
    rest = weighted * placing
    for i in range(TERMS):
        term = rest.astype(jnp.bfloat16)
        table[i] = term
        rest = rest - term.astype(jnp.float32)
    table[TERMS] = placing.astype(jnp.bfloat16)

    def sent(ref, count, sem):
        if count:
            part = ref.at[pl.ds(0, count)]
            pltpu.make_async_copy(part, part, sem).wait()

    def z_wait(s):
        z_copy(s, t, 0).wait_recv()

    def z_pass(i):
        held = order[i][1]
        for s, to in relay[i]:
            if s != held:
                z_wait(s)
            held = s
            z_copy(s, to, 1).start()

    def z_drain(i):
        sent(tokens_in, len(own[i]), z_send.at[0])
        sent(tokens_in, len(relay[i]), z_send.at[1])

    def place(b, s, source):
        return (b * nt + s) * ne + source

    def f_copy(s, j, k):
        chip = lax.rem(e // PAIR + k // PAIR, nx)
        to = chip * PAIR + lax.rem(e + k, PAIR)
        return pltpu.make_async_remote_copy(
            src_ref=packed.at[s, to],
            dst_ref=feats.at[place(d, s, e)],
            send_sem=f_send.at[0],
            recv_sem=f_recv.at[d, s, e // PAIR],
            device_id=(lax.rem(d + j, nd), to, t),
            device_id_type=MESH,
        )

    def spread(s):
        packed[s] = (
            jnp.dot(table[TERMS], tokens_in[s], preferred_element_type=jnp.float32)
            .astype(jnp.bfloat16)
            .reshape(ne, CAP, width)
        )
        for k in range(1, ne):
            f_copy(s, 0, k).start()
        for j in range(1, nd):
            for k in range(PAIR):
                f_copy(s, j, k).start()
        feats[place(d, s, e)] = packed[s, e]

    def spread_far(s):
        for j in range(1, nd):
            for k in range(PAIR, ne):
                f_copy(s, j, k).start()

    def f_arrive(g, s):
        b, base = group(g)
        count = PAIR - 1 if isinstance(g, int) and g == 0 else PAIR
        block = feats.at[pl.ds(place(b, s, base), count)]
        pltpu.make_async_copy(block, block, f_recv.at[b, s, base // PAIR]).wait()

    def gate_up(gs, k, p=None):
        s = shard[k]
        columns = slice(None) if p is None else slice(p * share, (p + 1) * share)
        x = [
            feats[pl.ds(place(b, s, base), PAIR)].reshape(rows, width)
            for b, base in map(group, gs)
        ]
        x = jnp.concatenate(x) if len(gs) > 1 else x[0]
        here = slice(0, rows * len(gs))
        gate = jnp.dot(x, gate_up_w[s, 0, :, columns], preferred_element_type=jnp.float32)
        up = jnp.dot(x, gate_up_w[s, 1, :, columns], preferred_element_type=jnp.float32)
        if k == 0:
            gate_acc[here, columns] = gate
            up_acc[here, columns] = up
        else:
            gate_acc[here, columns] += gate
            up_acc[here, columns] += up

    def unit_place(b, s, base):
        return (b * nt + s) * nx + base // PAIR

    def activate(gs, p):
        for i, g in enumerate(gs):
            b, base = group(g)
            here, columns = pl.ds(i * rows, rows), pl.ds(p * share, share)
            gate = gate_acc[here, columns]
            value = gate / (1.0 + jnp.exp(-gate)) * up_acc[here, columns]
            acts[unit_place(b, t, base), p] = value.astype(jnp.bfloat16)
            u_own(g, p)

    def u_copy(g, s, to, sem, p=None):
        b, base = group(g)
        block = acts.at[unit_place(b, s, base)]
        if p is not None:
            block = block.at[p]
        return pltpu.make_async_remote_copy(
            src_ref=block,
            dst_ref=block,
            send_sem=u_send.at[sem],
            recv_sem=u_recv.at[g, s],
            device_id=(d, e, to),
            device_id_type=MESH,
        )

    def patient(i):
        return [to for to in own[i] if i in (0, nt - 1) and abs(to - i) == 1 and len(own[i]) > 1]

    def u_own(g, p):
        def act(i):
            for to in own[i]:
                if to not in patient(i):
                    u_copy(g, i, to, 0, p).start()

        per_place(act)

    def u_late(gs):
        def act(i):
            for g in gs:
                for to in patient(i):
                    u_copy(g, i, to, 0).start()

        per_place(act)

    def u_pass(gs, near):
        def act(i):
            for g in gs:
                held = None
                for s, to in relay[i]:
                    if (abs(s - i) == 1) == near:
                        copy = u_copy(g, s, to, 1)
                        if s != held:
                            copy.wait_recv()
                        held = s
                        copy.start()

        with jax.named_scope("pass_near" if near else "pass_far"):
            per_place(act)

    def u_take(g, s, skip):
        @pl.when(skip == 0)
        def _():
            u_copy(g, s, t, 0).wait_recv()

    def u_drain(i):
        sent(acts, groups * len(own[i]), u_send.at[0])
        sent(acts, groups * len(relay[i]), u_send.at[1])

    def down(gs, s, first, columns=slice(None)):
        h = [
            jnp.concatenate([acts[unit_place(b, s, base), p] for p in range(parts)], axis=1)
            for b, base in map(group, gs)
        ]
        h = jnp.concatenate(h) if len(gs) > 1 else h[0]
        value = jnp.dot(h, down_w[s, :, columns], preferred_element_type=jnp.float32)
        for i, g in enumerate(gs):
            part = value[i * rows : (i + 1) * rows]
            if first:
                down_acc[g, :, columns] = part
            else:
                down_acc[g, :, columns] += part

    def ret_copy(g, c, columns):
        b, base = group(g)
        return pltpu.make_async_remote_copy(
            src_ref=outgoing.at[b * ne + base + c, :, columns],
            dst_ref=returned.at[d * ne + e, :, columns],
            send_sem=ret_send.at[0],
            recv_sem=ret_recv.at[d, e // PAIR],
            device_id=(b, base + c, t),
            device_id_type=MESH,
        )

    def give_back(g, start=0, size=width):
        b, base = group(g)
        columns = pl.ds(start, size)
        first = pl.multiple_of(b * ne + base, PAIR)
        outgoing[pl.ds(first, PAIR), :, columns] = (
            down_acc[g, :, columns].astype(jnp.bfloat16).reshape(PAIR, CAP, size)
        )
        for c in range(PAIR):
            here = (b == d) & (base + c == e)

            @pl.when(jnp.logical_not(here))
            def _():
                ret_copy(g, c, columns).start()

            @pl.when(here)
            def _():
                returned[d * ne + e, :, columns] = outgoing[d * ne + e, :, columns]

    def ret_arrive(g, count):
        b, base = group(g)
        block = returned.at[pl.ds(b * ne + base, count)]
        pltpu.make_async_copy(block, block, ret_recv.at[b, base // PAIR]).wait()

    spread(t)
    spread_far(t)

    def first_batch(k):
        with jax.named_scope("f_arrive"):
            f_arrive(0, shard[k])
        with jax.named_scope("w_arrive"):
            pltpu.make_async_copy(
                gate_up_w.at[shard[k]], gate_up_w.at[shard[k]], w_sem.at[shard[k]]
            ).wait()
        for p in range(parts) if k == nt - 1 else (None,):
            with jax.named_scope("gate_up"):
                gate_up((0,), k, p)
            if p is not None:
                with jax.named_scope("activate"):
                    activate((0,), p)

    first_batch(0)
    busy = functools.reduce(jnp.logical_or, [t == i for i in range(nt) if relay[i]], t < 0)
    with jax.named_scope("z_arrive"):
        z_wait(shard[1])
        per_place(z_pass)
    with jax.named_scope("spread"):
        spread(shard[1])

    @pl.when(jnp.logical_not(busy))
    def _():
        first_batch(1)

    for k in range(2, nt):
        with jax.named_scope("z_arrive"):
            @pl.when(passed[k] == 0)
            def _():
                z_wait(shard[k])
        with jax.named_scope("spread"):
            spread(shard[k])

    @pl.when(busy)
    def _():
        first_batch(1)

    for k in range(2, nt):
        first_batch(k)
    for k in range(1, nt):
        spread_far(shard[k])

    def later_batch(index, gs):
        for p in range(parts):
            for k in range(nt):
                if p == 0:
                    with jax.named_scope("f_arrive"):
                        for g in gs:
                            f_arrive(g, shard[k])
                with jax.named_scope("gate_up"):
                    gate_up(gs, k, p)
                if p == 0 and k == nt - 2:
                    @pl.when(index == 2)
                    def _():
                        u_pass((0,), False)

                    @pl.when(index > 2)
                    def _():
                        of_batch(index - 2, lambda old: u_pass(old, True))
            with jax.named_scope("activate"):
                activate(gs, p)
        of_batch(index - 1, u_late)

        @pl.when(index == 1)
        def _():
            u_pass((0,), True)

        if not listed:
            @pl.when(index > 1)
            def _():
                of_batch(index - 1, lambda old: u_pass(old, False))

    def pair_batch(index, carry):
        later_batch(index, (2 * index - 1, 2 * index))
        return carry

    lax.fori_loop(1, (groups + 1) // 2, pair_batch, 0)
    if groups % 2 == 0:
        later_batch(batches - 1, (groups - 1,))
    of_batch(batches - 1, u_late)

    pltpu.make_async_copy(down_w, down_w, w_sem.at[nt]).wait()

    def finish(q, carry):
        if batches > 1:
            @pl.when(q == 2)
            def _():
                of_batch(batches - 2, lambda gs: u_pass(gs, batches > 2))

        @pl.when(q == min(3, batches))
        def _():
            of_batch(batches - 1, lambda gs: u_pass(gs, True))

        @pl.when(q == min(3, batches))
        def _():
            of_batch(batches - 1, lambda gs: u_pass(gs, False))

        def step(k, gs):
            if k:
                with jax.named_scope("u_arrive%d" % k):
                    for g in gs:
                        u_take(g, shard[k], passed[k])
            with jax.named_scope("down"):
                down(gs, shard[k], k == 0)
            if k == nt - 1:
                for g in gs:
                    give_back(g)

        for k in range(nt):
            @pl.when((q >= k) & (q - k < batches))
            def _():
                of_batch(q - k, functools.partial(step, k))

        return carry

    def listed_step(index, end_k, mid_k, last):
        gs = ((0,), (1, 2), (3,))[index]
        s = jnp.where(at_end, shard[end_k], shard[mid_k])
        if end_k:
            with jax.named_scope("u_arrive%d%d%d" % (index, end_k, mid_k)):
                for g in gs:
                    u_take(g, s, jnp.where(at_end, 0, passed[mid_k]))
        with jax.named_scope("down"):
            cuts = 2 if last and index and width % 256 == 0 else 1
            for c in range(cuts):
                size = width // cuts
                down(gs, s, end_k == 0, slice(c * size, (c + 1) * size))
                if last:
                    for g in gs:
                        give_back(g, c * size, size)

    if listed:
        for index in range(3):
            listed_step(index, 0, 0, False)
        middle, final = (1, 2), (3,)
        u_pass(middle, False)
        listed_step(0, 1, 1, False)
        listed_step(1, 1, 3, False)

        @pl.when(jnp.logical_not(far_corner))
        def _():
            u_pass(middle, True)

        listed_step(0, 3, 3, False)
        listed_step(0, 2, 2, True)

        @pl.when(jnp.logical_not(far_corner))
        def _():
            listed_step(1, 3, 1, False)
            u_pass(final, True)
            listed_step(2, 1, 1, False)
            u_pass(final, False)
            listed_step(1, 2, 2, True)
            listed_step(2, 2, 3, False)
            listed_step(2, 3, 2, True)

        @pl.when(far_corner)
        def _():
            u_pass(final, True)
            listed_step(2, 1, 1, False)
            u_pass(final, False)
            listed_step(2, 2, 3, False)
            u_pass(middle, True)
            listed_step(2, 3, 2, True)
            listed_step(1, 3, 1, False)
            listed_step(1, 2, 2, True)
    else:
        lax.fori_loop(0, batches + nt - 1, finish, 0)

    total[...] = jnp.zeros((tokens, width), jnp.float32)

    def combine(g):
        with jax.named_scope("ret_arrive"):
            ret_arrive(g, PAIR - 1 if isinstance(g, int) else PAIR)
        with jax.named_scope("combine"):
            b, base = group(g)
            back = returned[pl.ds(b * ne + base, PAIR)].reshape(rows, width)
            places = pl.ds(pl.multiple_of(base * CAP, rows), rows)
            shares = jnp.concatenate([table[i, places] for i in range(TERMS)])
            total[...] += lax.dot_general(
                shares, jnp.concatenate([back] * TERMS), (((0,), (0,)), ((), ())),
                preferred_element_type=jnp.float32,
            )

    combine(0)
    corner = lax.rem(nd - 1 - d, nd) * nx + lax.rem(nx - 1 - e // PAIR, nx)
    corner = jnp.where(corner == 0, groups - 1, corner)

    def combine_next(i, carry):
        combine(1 + lax.rem(corner - 1 + i, groups - 1))
        return carry

    lax.fori_loop(1, groups, combine_next, 0)
    out_ref[...] = total[...].astype(jnp.bfloat16)

    with jax.named_scope("drain"):
        per_place(z_drain)
        sent(feats, nt * (nd * ne - 1), f_send.at[0])
        per_place(u_drain)
        sent(outgoing, nd * ne - 1, ret_send.at[0])


def body(mesh, hidden_states, chosen_experts, choice_weights, gate_proj, up_proj, down_proj):
    nd, ne, nt = mesh.shape["dp"], mesh.shape["expert"], mesh.shape["tensor"]
    tokens, width = hidden_states.shape
    units = gate_proj.shape[2]
    slots = ne * CAP
    rows = PAIR * CAP
    groups = nd * ne // PAIR
    parts = 1 if units % 256 else 2
    vmem = pl.BlockSpec(memory_space=pltpu.VMEM)
    hbm = pl.BlockSpec(memory_space=pltpu.HBM)
    bf16, f32, dma = jnp.bfloat16, jnp.float32, pltpu.SemaphoreType.DMA
    operands = [
        pltpu.with_memory_space_constraint(x, pltpu.HBM)
        for x in (hidden_states, chosen_experts.T, choice_weights.T, gate_proj, up_proj, down_proj)
    ]
    return pl.pallas_call(
        functools.partial(kernel, nd, ne, nt),
        out_shape=jax.ShapeDtypeStruct((tokens, width), bf16),
        in_specs=[hbm] * 6,
        out_specs=vmem,
        scratch_shapes=[
            pltpu.VMEM((nt, tokens, width), bf16),
            pltpu.VMEM(chosen_experts.shape[::-1], jnp.int32),
            pltpu.VMEM(choice_weights.shape[::-1], f32),
            pltpu.VMEM((nt, ne, CAP, width), bf16),
            pltpu.VMEM((nd * nt * ne, CAP, width), bf16),
            pltpu.VMEM((groups * nt, parts, rows, units // parts), bf16),
            pltpu.VMEM((nt, 2, width, units), bf16),
            pltpu.VMEM((nt, units, width), bf16),
            pltpu.VMEM((2 * rows, units), f32),
            pltpu.VMEM((2 * rows, units), f32),
            pltpu.VMEM((groups, rows, width), f32),
            pltpu.VMEM((nd * ne, CAP, width), bf16),
            pltpu.VMEM((nd * ne, CAP, width), bf16),
            pltpu.VMEM((TERMS + 1, slots, tokens), bf16),
            pltpu.VMEM((tokens, width), f32),
            dma((3,)),
            dma((nt + 1,)),
            dma((2,)),
            dma((nt,)),
            dma((1,)),
            dma((nd, nt, ne // PAIR)),
            dma((2,)),
            dma((groups, nt)),
            dma((1,)),
            dma((nd, ne // PAIR)),
        ],
        compiler_params=pltpu.CompilerParams(
            collective_id=0, has_side_effects=True, vmem_limit_bytes=48 << 20
        ),
        name="experts",
    )(*operands)


def solution(mesh):
    in_specs = (
        P(("dp", "expert"), "tensor"),
        P(("dp", "expert"), None),
        P(("dp", "expert"), None),
        P("expert", None, ("dp", "tensor")),
        P("expert", None, ("dp", "tensor")),
        P("expert", "dp", "tensor"),
    )
    out_specs = P(("dp", "expert"), "tensor")
    return jax.shard_map(
        functools.partial(body, mesh), mesh=mesh, in_specs=in_specs, out_specs=out_specs,
        check_vma=False,
    )
```
